32 devices in a mesh: dp: 8 (over z, x), mp: 4 (over y, core).
Axes of the slice: x: 2, y: 2, z: 4, core: 2. Of those that a mesh axis runs over, the one named last changes fastest.
Arguments:
- tokens: bfloat16 [256, 48, 3584], P('dp', None, 'mp'), may hold values from -180 to 180
- norm_gain: float32 [3584], replicated, may hold values from 0.1 to 1.9
- w_query: bfloat16 [3584, 3584], P('dp', 'mp'), may hold values from -0.16 to 0.16
- w_keyval: bfloat16 [3584, 2, 512], P('dp', None, 'mp'), may hold values from -0.16 to 0.16
- w_out: bfloat16 [3584, 3584], P('mp', 'dp'), may hold values from -0.09375 to 0.09375
- residents: bfloat16 [8, 2048, 3584], P('dp', 'mp'), may hold values from -6 to 6
- lengths: int32 [256], P('dp'), may hold values from 6 to 48
- cluster: int32 [256, 1], P('dp'), may hold values from 0 to 7; in each aligned block of 32 rows (0 to 31, 32 to 63, ...) at most 4 rows name the same one
- owner: int32 [8], replicated, may hold values from 0 to 7, each once
- counts: int32 [8], replicated, may hold values from 256 to 2048
- flags: int32 [256], P('dp'), may hold values 0 or 1
Outputs:
- similarity: float32 [256, 2048], P('dp', 'mp')
The draws below stay inside these ranges and needn't reach their ends.
Inputs may be any that keep to these rules, and one draw needn't show every extreme that they name: Each dialogue's cluster; among the 32 dialogues of one index of dp (aligned blocks of rows) no cluster is named more than 4 times. owner gives every cluster a distinct index of dp that holds its residents.
All inputs are finite; a program needn't handle non-finite values. No bound on the sum of `flags` on one device may be relied on, other than what follows from the above.
Results may differ from the reference program's by a relative error of at most 0.013.
Values may be sent and summed in bfloat16 or wider, within the bound.
A program may use at most 128 MiB of HBM per device.

```python
import math
import jax
import jax.numpy as jnp
import numpy as np
from jax import lax

D = 3584
HEADS = 28
KV_HEADS = 4
HEAD_DIM = 128
LEN = 48
MEMBERS = 2048
DLG_DEV = 32
DIALOGUES = 256
CLUSTERS = 8
CAP = 4


def draw_w_query(key, part):
    spread_scale = D ** (-0.5)
    noise_key = jax.random.fold_in(key, 11)
    shape_full = (D, HEADS * HEAD_DIM)
    drawn = jnp.clip(jax.random.normal(noise_key, shape_full, jnp.float32), -6.0, 6.0) * spread_scale
    return drawn.astype(jnp.bfloat16)


def draw_w_keyval(key, part):
    spread_scale = D ** (-0.5)
    noise_key = jax.random.fold_in(key, 13)
    shape_full = (D, 2, KV_HEADS * HEAD_DIM)
    drawn = jnp.clip(jax.random.normal(noise_key, shape_full, jnp.float32), -6.0, 6.0) * spread_scale
    return drawn.astype(jnp.bfloat16)


def draw_tokens(key, part):
    noise_key = jax.random.fold_in(key, 17)
    shape_full = (DIALOGUES, LEN, D)
    drawn = jnp.clip(jax.random.normal(noise_key, shape_full, jnp.float32), -6.0, 6.0)
    return drawn.astype(jnp.bfloat16)


def set_ends(array, rng, least, top_value):
    extent = array.shape
    index_at = [jax.random.randint(jax.random.fold_in(rng, axis), (), 0, extent[axis]) for axis in range(len(extent))]
    array = array.at[tuple(index_at)].set(least)
    longest = extent.index(max(extent))
    index_at[longest] = (index_at[longest] + 1) % extent[longest]
    return array.at[tuple(index_at)].set(top_value)


def levels(stream_key, shape, split, least, largest):
    loudness = 1.0
    for axis_at, blocks in split:
        steps = jax.random.uniform(jax.random.fold_in(jax.random.fold_in(stream_key, 6), axis_at), (blocks,), jnp.float32, least / len(split), largest / len(split))
        loudness = loudness * jnp.repeat(jnp.exp(steps), shape[axis_at] // blocks).reshape((-1,) + (1,) * (len(shape) - 1 - axis_at))
    return loudness


def assign_block(own_key, own, number, rows, amount, top, reach, skew):
    sequence = jax.random.permutation(own_key, amount)
    packed, usual = portions_of(amount, rows * top, reach, skew, True), portions_of(amount, rows * top, reach, skew, False)
    places = jnp.arange(amount)

    def named(sizes, rotation):
        used = int((sizes > 0).sum())
        fixed = max(1, used // 4)
        shifted = fixed + (places - fixed + rotation * (used - fixed)) % max(1, amount - fixed)
        return jnp.zeros((amount,), jnp.int32).at[sequence[jnp.where(places < fixed, places, shifted)]].set(jnp.asarray(sizes, jnp.int32))

    sizes = jnp.where(number % 4 == 0, named(packed, number // 4), named(usual, number - number // 4 - 1))
    mixed = jax.random.permutation(jax.random.fold_in(own, 3), amount)
    source_of, receiver = mixed[0:amount // 2 * 2:2], mixed[1:amount // 2 * 2:2]
    margin = jnp.minimum(sizes[source_of] - 1, reach - sizes[receiver]) // 2
    margin = jnp.where((source_of == sequence[0]) | (receiver == sequence[0]) | (sizes[receiver] == 0), 0, jnp.maximum(margin, 0))
    shifted = jax.random.randint(jax.random.fold_in(own, 4), (amount // 2,), 0, 1 << 20) % (margin + 1)
    sizes = sizes.at[source_of].add(-shifted).at[receiver].add(shifted)
    items = jnp.searchsorted(jnp.cumsum(sizes), jnp.arange(rows * top), side="right").astype(jnp.int32)
    listing = items.reshape(top, rows).T
    listing = listing[jax.random.permutation(jax.random.fold_in(own, 1), rows)]
    rotation = jax.random.randint(jax.random.fold_in(own, 2), (rows, 1), 0, top)
    return jnp.take_along_axis(listing, (jnp.arange(top)[None, :] + rotation) % top, axis=1)


def portions_of(amount, total, bound, skew, full):
    portions = [(1 << 20) // math.isqrt(rank ** skew) + 1 for rank in range(1, amount + 1)]
    largest = bound if full else min(bound, max(-(-total // amount), total * portions[0] // sum(portions)))
    least = 1 if total - largest >= amount - 1 else 0
    holding, rest = [largest] + [least] * (amount - 1), total - largest - least * (amount - 1)
    while rest > 0:
        free = [i for i in range(1, amount) if holding[i] < largest] or [i for i in range(1, amount) if holding[i] < bound]
        pool, left = sum([portions[i] for i in free]), rest
        for i in free:
            more = min(bound - holding[i], max(1, left * portions[i] // pool), rest)
            holding[i] = holding[i] + more
            rest = rest - more
    return np.array(holding)


def scatter_about(stream_key, shape, scale, most, pieces=(), kind=jnp.bfloat16):
    loudness = levels(stream_key, shape, pieces, -0.22, 0.18) if pieces else 1.0
    array = jax.random.normal(stream_key, shape, jnp.float32) * scale * loudness
    return jnp.minimum(jnp.maximum(array, -most), most).astype(kind)


def setup_inputs(seed: int = 0) -> dict:
    key_of = jax.random.split(jax.random.key(seed), 12)
    tokens = draw_tokens(jax.random.fold_in(key_of[11], 71), 0)
    norm_gain = jnp.clip(1.0 + 0.18 * jax.random.normal(key_of[1], (D,), jnp.float32), 0.1, 1.9)
    w_query = draw_w_query(jax.random.fold_in(key_of[11], 71), 0)
    w_keyval = draw_w_keyval(jax.random.fold_in(key_of[11], 71), 0)
    w_out = scatter_about(key_of[4], (HEADS * HEAD_DIM, D), (HEADS * HEAD_DIM) ** -0.5, 0.09375, ((0, 4), (1, 8)))
    residents = scatter_about(key_of[5], (CLUSTERS, MEMBERS, D), 1.0, 6.0, ((0, 8), (1, 4)))
    lengths = set_ends(jax.random.randint(key_of[6], (DIALOGUES,), LEN // 8, LEN + 1), jax.random.fold_in(key_of[6], 1), LEN // 8, LEN).astype(jnp.int32)
    cluster_keys = jax.random.split(jax.random.fold_in(key_of[7], 1), DIALOGUES // DLG_DEV)
    cluster_turns = jax.random.permutation(jax.random.fold_in(key_of[7], 3), DIALOGUES // DLG_DEV)
    cluster = jax.vmap(lambda own, number: assign_block(jax.random.fold_in(key_of[7], 2), own, number, DLG_DEV, CLUSTERS, 1, CAP, 2))(cluster_keys, cluster_turns).reshape((DIALOGUES, 1))
    owner = jax.random.permutation(key_of[8], CLUSTERS).astype(jnp.int32)
    counts = set_ends(jax.random.randint(key_of[9], (CLUSTERS,), MEMBERS // 8, MEMBERS + 1), jax.random.fold_in(key_of[9], 1), MEMBERS // 8, MEMBERS).astype(jnp.int32)
    flags = set_ends((jax.random.randint(key_of[10], (DIALOGUES,), 0, 4) < 3).astype(jnp.int32), jax.random.fold_in(key_of[10], 1), 0, 1)
    return {"tokens": tokens, "norm_gain": norm_gain, "w_query": w_query, "w_keyval": w_keyval, "w_out": w_out, "residents": residents, "lengths": lengths, "cluster": cluster, "owner": owner, "counts": counts, "flags": flags}


rope_base = 1000000.0
logit_scale = 100.0

def rotate(values, positions):
    half = values.shape[-1] // 2
    freqs = rope_base ** (-jnp.arange(half, dtype=jnp.float32) * 2.0 / values.shape[-1])
    angles = positions.astype(jnp.float32)[:, None] * freqs[None, :]
    cosine = jnp.cos(angles)[:, None, :]
    sine = jnp.sin(angles)[:, None, :]
    first = values[..., :half]
    second = values[..., half:]
    return jnp.concatenate([first * cosine - second * sine, second * cosine + first * sine], axis=-1)

def attend(query, keys, values, length):
    seq_len = query.shape[0]
    kv_count = keys.shape[1]
    group = query.shape[1] // kv_count
    grouped = query.reshape(seq_len, kv_count, group, query.shape[-1]).astype(jnp.float32)
    scores = jnp.einsum('qkgd,pkd->kgqp', grouped, keys.astype(jnp.float32)) / math.sqrt(query.shape[-1])
    row_pos = jnp.arange(seq_len)[:, None]
    col_pos = jnp.arange(seq_len)[None, :]
    allowed = (col_pos <= row_pos) & (col_pos < length)
    scores = jnp.where(allowed, scores, -1e+30)
    highest = lax.optimization_barrier(jnp.max(scores, axis=-1, keepdims=True))
    expanded = jnp.exp(scores - highest)
    weights = (expanded / lax.optimization_barrier(jnp.sum(expanded, axis=-1, keepdims=True))).astype(jnp.bfloat16)
    context = jnp.einsum('kgqp,pkd->qkgd', weights.astype(jnp.float32), values.astype(jnp.float32))
    valid = (jnp.arange(seq_len) < length).astype(jnp.float32)
    pooled = lax.optimization_barrier(jnp.sum(context * valid[:, None, None, None], axis=0)) / length.astype(jnp.float32)
    return pooled.reshape(-1)

def reference(tokens, norm_gain, w_query, w_keyval, w_out, residents, lengths, cluster, owner, counts, flags):
    keyval_flat = w_keyval.reshape(D, 2 * KV_HEADS * HEAD_DIM)
    positions = jnp.arange(LEN)

    def one_dialogue(inputs):
        dialogue, length = inputs
        hidden = dialogue.astype(jnp.float32)
        normed = (hidden * lax.rsqrt(lax.optimization_barrier(jnp.mean(hidden * hidden, axis=-1, keepdims=True)) + 1e-06) * norm_gain).astype(jnp.bfloat16)
        query = jnp.dot(normed, w_query, preferred_element_type=jnp.float32).reshape(LEN, HEADS, HEAD_DIM)
        keyval = jnp.dot(normed, keyval_flat, preferred_element_type=jnp.float32).reshape(LEN, 2, KV_HEADS, HEAD_DIM)
        query = rotate(query, positions).astype(jnp.bfloat16)
        keys = rotate(keyval[:, 0], positions).astype(jnp.bfloat16)
        values = keyval[:, 1].astype(jnp.bfloat16)
        context = attend(query, keys, values, length).astype(jnp.bfloat16)
        valid = (positions < length).astype(jnp.float32)
        pooled_input = lax.optimization_barrier(jnp.sum(hidden * valid[:, None], axis=0)) / length.astype(jnp.float32)
        return (context, pooled_input)
    pooled_context, pooled_input = lax.map(one_dialogue, (tokens, lengths))
    embedding = pooled_input + jnp.dot(pooled_context, w_out, preferred_element_type=jnp.float32)
    unit = embedding * lax.rsqrt(lax.optimization_barrier(jnp.sum(embedding * embedding, axis=-1, keepdims=True)) + 1e-06)
    unit = (unit * flags.astype(jnp.float32)[:, None]).astype(jnp.bfloat16)

    def resident_norm(members):
        wide = members.astype(jnp.float32)
        return lax.rsqrt(lax.optimization_barrier(jnp.sum(wide * wide, axis=-1)) + 1e-06)
    inverse_norm = lax.map(resident_norm, residents)
    cluster_ids = cluster[:, 0].astype(jnp.int32)
    slots = owner[cluster_ids].astype(jnp.int32)
    limits = counts[cluster_ids]

    def one_row(inputs):
        query_unit, slot, limit = inputs
        members = lax.dynamic_index_in_dim(residents, slot, 0, keepdims=False)
        dots = jnp.dot(members, query_unit, preferred_element_type=jnp.float32)
        scale_row = lax.dynamic_index_in_dim(inverse_norm, slot, 0, keepdims=False)
        live = jnp.arange(MEMBERS) < limit
        return jnp.where(live, logit_scale * dots * scale_row, 0.0)
    return lax.map(one_row, (unit, slots, limits))
```

```python
import math

import jax
import jax.numpy as jnp
from jax import lax
from jax.experimental import pallas as pl
from jax.experimental.pallas import tpu as pltpu
from jax.sharding import PartitionSpec as P

HEAD_DIM = 128


rope_base = 1000000.0
logit_scale = 100.0


def rotate(values, positions):
    half = values.shape[-1] // 2
    freqs = rope_base ** (-jnp.arange(half, dtype=jnp.float32) * 2.0 / values.shape[-1])
    angles = positions.astype(jnp.float32)[:, None] * freqs[None, :]
    cosine = jnp.cos(angles)[:, None, :]
    sine = jnp.sin(angles)[:, None, :]
    first = values[..., :half]
    second = values[..., half:]
    return jnp.concatenate(
        [first * cosine - second * sine, second * cosine + first * sine], axis=-1
    )


def attend(query, keys, values, length):
    seq_len = query.shape[0]
    kv_count = keys.shape[1]
    group = query.shape[1] // kv_count
    grouped = query.reshape(seq_len, kv_count, group, query.shape[-1])
    scores = jnp.einsum(
        "qkgd,pkd->kgqp", grouped, keys, preferred_element_type=jnp.float32
    ) / math.sqrt(query.shape[-1])
    row_pos = jnp.arange(seq_len)[:, None]
    col_pos = jnp.arange(seq_len)[None, :]
    allowed = (col_pos <= row_pos) & (col_pos < length)
    scores = jnp.where(allowed, scores, -1e30)
    highest = jnp.max(scores, axis=-1, keepdims=True)
    expanded = jnp.exp(scores - highest)
    weights = (expanded / jnp.sum(expanded, axis=-1, keepdims=True)).astype(jnp.bfloat16)
    context = jnp.einsum("kgqp,pkd->qkgd", weights, values, preferred_element_type=jnp.float32)
    valid = (jnp.arange(seq_len) < length).astype(jnp.float32)
    pooled = jnp.sum(context * valid[:, None, None, None], axis=0) / length.astype(jnp.float32)
    return pooled.reshape(-1)


MESH = pl.DeviceIdType.MESH
ROWS = 384


def gather_project_kernel(
    tin, win, gain, mask, cosine, sine, qkv, pooled,
    tok, wbuf, scaled, acc, squares,
    tsend, trecv, wsend, wrecv, lsem,
):
    dp = lax.axis_index("dp")
    mp = lax.axis_index("mp")
    z, x = dp // 2, dp % 2
    core_peer = mp + 1 - 2 * (mp % 2)
    y_peer = (mp + 2) % 4
    far = (core_peer + 2) % 4
    x_peer = 2 * z + 1 - x
    total = tin.shape[0]

    barrier = pltpu.get_barrier_semaphore()

    def greet(dp_to, mp_to):
        pl.semaphore_signal(
            barrier, inc=1, device_id={"dp": dp_to, "mp": mp_to}, device_id_type=MESH
        )

    greet(dp, core_peer)
    greet(dp, y_peer)
    greet(x_peer, mp)
    has_up, has_down = z < 3, z > 0

    @pl.when(has_up)
    def _():
        greet(dp + 2, mp)

    @pl.when(has_down)
    def _():
        greet(dp - 2, mp)

    @pl.when(has_up & has_down)
    def _():
        pl.semaphore_wait(barrier, 5)

    @pl.when(jnp.logical_not(has_up & has_down))
    def _():
        pl.semaphore_wait(barrier, 4)

    def token_copy(index, source, slot, mp_to):
        return pltpu.make_async_remote_copy(
            src_ref=source, dst_ref=tok.at[slot], send_sem=tsend.at[index],
            recv_sem=trecv.at[index], device_id={"dp": dp, "mp": mp_to}, device_id_type=MESH,
        )

    def weight_copy(way, z_from, source):
        slot = 2 * z_from + x
        dp_to = (dp + 2, dp - 2, x_peer)[way]
        return pltpu.make_async_remote_copy(
            src_ref=wbuf.at[slot] if source is None else source, dst_ref=wbuf.at[slot],
            send_sem=wsend.at[way, z_from], recv_sem=wrecv.at[slot],
            device_id={"dp": dp_to, "mp": mp}, device_id_type=MESH,
        )

    def weight_arrival(slot):
        pltpu.make_async_remote_copy(
            src_ref=wbuf.at[slot], dst_ref=wbuf.at[slot], send_sem=wsend.at[0, 0],
            recv_sem=wrecv.at[slot], device_id={"dp": x_peer, "mp": mp}, device_id_type=MESH,
        ).wait_recv()

    across = token_copy(0, tin, mp, y_peer)
    across.start()

    @pl.when(has_up)
    def _():
        weight_copy(0, z, win).start()

    @pl.when(has_down)
    def _():
        weight_copy(1, z, win).start()

    weight_copy(2, z, win).start()
    beside = token_copy(1, tin, mp, core_peer)
    beside.start()
    own = pltpu.make_async_copy(win, wbuf.at[dp], lsem)
    own.start()

    squares[...] = jnp.zeros_like(squares)

    def prepare(source, slot):
        @pl.loop(0, total // 96)
        def _(step):
            rows = pl.ds(pl.multiple_of(step * 96, 96), 96)
            values = source[rows, :].astype(jnp.float32)
            squares[rows, :] += jnp.sum(values * values, axis=-1, keepdims=True)
            scaled[slot, rows, :] = (values * gain[slot]).astype(jnp.bfloat16)

        pooled[slot] = jnp.dot(mask[...], source[...], preferred_element_type=jnp.float32)

    prepare(tin, mp)
    beside.wait_recv()
    prepare(tok.at[core_peer], core_peer)
    own.wait()

    def relay(k):
        @pl.when(z >= k)
        def _():
            weight_arrival(2 * (z - k) + x)

            @pl.when(has_up)
            def _():
                weight_copy(0, z - k, None).start()

            weight_copy(2, z - k, None).start()

        @pl.when(z + k <= 3)
        def _():
            weight_arrival(2 * (z + k) + x)

            @pl.when(has_down)
            def _():
                weight_copy(1, z + k, None).start()

            weight_copy(2, z + k, None).start()

    relay(1)
    relay(2)
    across.wait_recv()
    onward = token_copy(2, tok.at[y_peer], y_peer, core_peer)
    onward.start()
    relay(3)
    prepare(tok.at[y_peer], y_peer)
    onward.wait_recv()
    prepare(tok.at[far], far)

    width = 4 * tin.shape[1]
    columns = win.shape[1]

    def multiply(turn):
        block = (z, z + 1 - 2 * (z % 2), (z + 2) % 4, 3 - z)[turn]
        weight_arrival(2 * block + 1 - x)
        weights = wbuf.at[pl.ds(2 * block, 2)]

        @pl.loop(0, total // ROWS)
        def _(step):
            rows = pl.ds(pl.multiple_of(step * ROWS, ROWS), ROWS)
            product = jnp.dot(
                scaled[block, rows, :],
                weights[...].reshape(2 * win.shape[0], columns),
                preferred_element_type=jnp.float32,
            )
            if turn == 0:
                acc[rows, :] = product
            else:
                acc[rows, :] += product

    for turn in range(4):
        multiply(turn)

    @pl.loop(0, total // ROWS)
    def _(step):
        rows = pl.ds(pl.multiple_of(step * ROWS, ROWS), ROWS)
        scale = lax.rsqrt(squares[rows, :] * (1.0 / width) + 1e-06)
        for head in range(columns // HEAD_DIM):
            span = pl.ds(head * HEAD_DIM, HEAD_DIM)
            piece = acc[rows, span] * scale
            if head < columns // HEAD_DIM - 1:
                piece = piece * cosine[...] + pltpu.roll(piece, HEAD_DIM // 2, 1) * sine[...]
            qkv[rows, span] = piece.astype(jnp.bfloat16)

    across.wait_send()
    beside.wait_send()
    onward.wait_send()

    for z_from in range(4):
        @pl.when(has_up & (z >= z_from))
        def _():
            weight_copy(0, z_from, None).wait_send()

        @pl.when(has_down & (z <= z_from))
        def _():
            weight_copy(1, z_from, None).wait_send()

        weight_copy(2, z_from, None).wait_send()


def gather_project(tokens, norm_gain, w_query, w_keyval, lengths):
    dialogs, seq_len, part = tokens.shape
    total = dialogs * seq_len
    weights = jnp.concatenate([w_query, w_keyval.reshape(w_keyval.shape[0], -1)], axis=1)
    depth, columns = weights.shape
    positions = jnp.arange(seq_len)
    half = HEAD_DIM // 2
    freqs = rope_base ** (-jnp.arange(half, dtype=jnp.float32) * 2.0 / HEAD_DIM)
    angles = positions.astype(jnp.float32)[:, None] * freqs[None, :]
    cosine = jnp.cos(angles)
    sine = jnp.sin(angles)
    cosine = jnp.tile(jnp.concatenate([cosine, cosine], axis=1), (ROWS // seq_len, 1))
    sine = jnp.tile(jnp.concatenate([-sine, sine], axis=1), (ROWS // seq_len, 1))
    row = jnp.arange(total)[None, :]
    mine = jnp.arange(dialogs)[:, None]
    mask = ((row // seq_len == mine) & (row % seq_len < lengths[:, None])).astype(jnp.bfloat16)
    vmem = pl.BlockSpec(memory_space=pltpu.VMEM)
    qkv, pooled = pl.pallas_call(
        gather_project_kernel,
        out_shape=(
            jax.ShapeDtypeStruct((total, columns), jnp.bfloat16),
            jax.ShapeDtypeStruct((4, dialogs, part), jnp.float32),
        ),
        in_specs=[vmem] * 6,
        out_specs=(vmem, vmem),
        scratch_shapes=[
            pltpu.VMEM((4, total, part), jnp.bfloat16),
            pltpu.VMEM((8, depth, columns), jnp.bfloat16),
            pltpu.VMEM((4, total, part), jnp.bfloat16),
            pltpu.VMEM((total, columns), jnp.float32),
            pltpu.VMEM((total, 1), jnp.float32),
            pltpu.SemaphoreType.DMA((3,)),
            pltpu.SemaphoreType.DMA((3,)),
            pltpu.SemaphoreType.DMA((3, 4)),
            pltpu.SemaphoreType.DMA((8,)),
            pltpu.SemaphoreType.DMA,
        ],
        compiler_params=pltpu.CompilerParams(
            collective_id=0, has_side_effects=True, vmem_limit_bytes=58 * 1024 * 1024
        ),
    )(
        tokens.reshape(total, part), weights, norm_gain.reshape(4, 1, part), mask, cosine, sine
    )
    pooled_input = (pooled / lengths.astype(jnp.float32)[None, :, None]).transpose(1, 0, 2)
    queries = w_query.shape[1]
    shape = (dialogs, seq_len, -1, HEAD_DIM)
    return (
        qkv[:, :queries].reshape(shape),
        qkv[:, queries : queries + HEAD_DIM].reshape(shape),
        qkv[:, queries + HEAD_DIM :].reshape(shape),
        pooled_input.reshape(dialogs, 4 * part),
    )


def plain_project(tokens, norm_gain, w_query, w_keyval, lengths):
    gathered = lax.all_gather(tokens, "mp", axis=2, tiled=True)
    dialogs, seq_len, width = gathered.shape
    hidden = gathered.astype(jnp.float32)
    normed = (
        hidden * lax.rsqrt(jnp.mean(hidden * hidden, axis=-1, keepdims=True) + 1e-06) * norm_gain
    ).astype(jnp.bfloat16)
    normed_flat = normed.reshape(dialogs * seq_len, width)
    query_cols = w_query.shape[1]
    keyval_cols = w_keyval.shape[2]
    pieces = (
        lax.all_gather(w_query, "dp", axis=0, tiled=True),
        lax.all_gather(w_keyval, "dp", axis=0, tiled=True),
    )
    keyval_piece = pieces[1].reshape(pieces[1].shape[0], 2 * keyval_cols)
    query_sum = jnp.dot(normed_flat, pieces[0], preferred_element_type=jnp.float32)
    keyval_sum = jnp.dot(normed_flat, keyval_piece, preferred_element_type=jnp.float32)
    positions = jnp.arange(seq_len)
    local_heads = query_cols // HEAD_DIM
    local_kv = keyval_cols // HEAD_DIM
    query = jax.vmap(lambda block: rotate(block, positions))(
        query_sum.reshape(dialogs, seq_len, local_heads, HEAD_DIM)
    ).astype(jnp.bfloat16)
    keys = jax.vmap(lambda block: rotate(block, positions))(
        keyval_sum[:, :keyval_cols].reshape(dialogs, seq_len, local_kv, HEAD_DIM)
    ).astype(jnp.bfloat16)
    values = (
        keyval_sum[:, keyval_cols:]
        .reshape(dialogs, seq_len, local_kv, HEAD_DIM)
        .astype(jnp.bfloat16)
    )
    valid = (positions[None, :] < lengths[:, None]).astype(jnp.float32)
    pooled_input = (
        jnp.sum(hidden * valid[:, :, None], axis=1) / lengths.astype(jnp.float32)[:, None]
    )
    return query, keys, values, pooled_input


def local(
    tokens, norm_gain, w_query, w_keyval, w_out, residents, lengths, cluster, owner, counts, flags
):
    if lax.axis_size("dp") == 8 and lax.axis_size("mp") == 4:
        project = gather_project
    else:
        project = plain_project
    query, keys, values, pooled_input = project(tokens, norm_gain, w_query, w_keyval, lengths)
    dialogs = query.shape[0]
    pooled_context = jax.vmap(attend)(query, keys, values, lengths).astype(jnp.bfloat16)
    everyone = lax.all_gather(pooled_context, "dp", axis=0, tiled=True)
    slices = jnp.dot(everyone, w_out, preferred_element_type=jnp.float32).astype(jnp.bfloat16)
    slices = slices.reshape(-1, dialogs, w_out.shape[1])
    slices = lax.all_to_all(slices, "dp", split_axis=0, concat_axis=0, tiled=True)
    partial_out = slices.transpose(1, 0, 2).reshape(dialogs, -1)
    projected = lax.psum(partial_out, "mp").astype(jnp.float32)
    embedding = pooled_input + projected
    unit = embedding * lax.rsqrt(jnp.sum(embedding * embedding, axis=-1, keepdims=True) + 1e-06)
    unit = (unit * flags.astype(jnp.float32)[:, None]).astype(jnp.bfloat16)
    my_index = lax.axis_index("dp")
    owner_count = lax.axis_size("dp")
    my_count = jnp.sum(jnp.where(owner == my_index, counts, 0))
    members = residents[0]
    member_count = members.shape[0]
    inverse_norm = lax.rsqrt(
        jnp.einsum("md,md->m", members, members, preferred_element_type=jnp.float32) + 1e-06
    )
    member_start = lax.axis_index("mp") * member_count
    live = member_start + jnp.arange(member_count) < my_count
    table_size = owner.shape[0]
    cluster_ids = cluster[:, 0]
    destination = jnp.sum(
        jnp.where(jnp.arange(table_size)[None, :] == cluster_ids[:, None], owner[None, :], 0),
        axis=1,
    )
    capacity = max(1, -(-dialogs // owner_count))
    order = jnp.arange(dialogs)
    earlier = (destination[None, :] == destination[:, None]) & (order[None, :] < order[:, None])
    rank = jnp.sum(earlier.astype(jnp.int32), axis=1)
    onehot = (jnp.arange(owner_count)[:, None, None] == destination[None, None, :]) & (
        jnp.arange(capacity)[None, :, None] == rank[None, None, :]
    )
    outgoing = jnp.einsum(
        "ocn,nd->ocd", onehot.astype(jnp.bfloat16), unit, preferred_element_type=jnp.float32
    ).astype(jnp.bfloat16)
    query_rows = lax.all_to_all(outgoing, "dp", split_axis=0, concat_axis=0, tiled=True)
    dots = lax.dot_general(
        query_rows,
        members,
        (((query_rows.ndim - 1,), (1,)), ((), ())),
        preferred_element_type=jnp.float32,
    )
    returned = lax.all_to_all(
        jnp.where(live, logit_scale * dots * inverse_norm, 0.0).astype(jnp.bfloat16),
        "dp",
        split_axis=0,
        concat_axis=0,
        tiled=True,
    ).astype(jnp.float32)
    similarity = jnp.einsum(
        "ocn,ocm->nm", onehot.astype(jnp.float32), returned, precision=lax.Precision.HIGHEST
    )
    return similarity


def solution(mesh):
    in_specs = (
        P("dp", None, "mp"),
        P(),
        P("dp", "mp"),
        P("dp", None, "mp"),
        P("mp", "dp"),
        P("dp", "mp", None),
        P("dp"),
        P("dp", None),
        P(),
        P(),
        P("dp"),
    )
    out_specs = P("dp", "mp")
    return jax.shard_map(local, mesh=mesh, in_specs=in_specs, out_specs=out_specs, check_vma=False)
```

```python
import math

import jax
import jax.numpy as jnp
from jax import lax
from jax.experimental import pallas as pl
from jax.experimental.pallas import tpu as pltpu
from jax.sharding import PartitionSpec as P

HEAD_DIM = 128


rope_base = 1000000.0
logit_scale = 100.0


def rotate(values, positions):
    half = values.shape[-1] // 2
    freqs = rope_base ** (-jnp.arange(half, dtype=jnp.float32) * 2.0 / values.shape[-1])
    angles = positions.astype(jnp.float32)[:, None] * freqs[None, :]
    cosine = jnp.cos(angles)[:, None, :]
    sine = jnp.sin(angles)[:, None, :]
    first = values[..., :half]
    second = values[..., half:]
    return jnp.concatenate(
        [first * cosine - second * sine, second * cosine + first * sine], axis=-1
    )


def attend(query, keys, values, length):
    seq_len = query.shape[0]
    kv_count = keys.shape[1]
    group = query.shape[1] // kv_count
    grouped = query.reshape(seq_len, kv_count, group, query.shape[-1])
    scores = jnp.einsum(
        "qkgd,pkd->kgqp", grouped, keys, preferred_element_type=jnp.float32
    ) / math.sqrt(query.shape[-1])
    row_pos = jnp.arange(seq_len)[:, None]
    col_pos = jnp.arange(seq_len)[None, :]
    allowed = (col_pos <= row_pos) & (col_pos < length)
    scores = jnp.where(allowed, scores, -1e30)
    highest = jnp.max(scores, axis=-1, keepdims=True)
    expanded = jnp.exp(scores - highest)
    weights = (expanded / jnp.sum(expanded, axis=-1, keepdims=True)).astype(jnp.bfloat16)
    context = jnp.einsum("kgqp,pkd->qkgd", weights, values, preferred_element_type=jnp.float32)
    valid = (jnp.arange(seq_len) < length).astype(jnp.float32)
    pooled = jnp.sum(context * valid[:, None, None, None], axis=0) / length.astype(jnp.float32)
    return pooled.reshape(-1)


MESH = pl.DeviceIdType.MESH
ROWS = 384


def gather_project_kernel(
    tin, win, gain, mask, cosine, sine, qkv, pooled,
    tok, wbuf, scaled, acc, squares,
    tsend, trecv, wsend, wrecv, lsem,
):
    dp = lax.axis_index("dp")
    mp = lax.axis_index("mp")
    z, x = dp // 2, dp % 2
    core_peer = mp + 1 - 2 * (mp % 2)
    y_peer = (mp + 2) % 4
    far = (core_peer + 2) % 4
    x_peer = 2 * z + 1 - x
    total = tin.shape[0]

    barrier = pltpu.get_barrier_semaphore()

    def greet(dp_to, mp_to):
        pl.semaphore_signal(
            barrier, inc=1, device_id={"dp": dp_to, "mp": mp_to}, device_id_type=MESH
        )

    greet(dp, core_peer)
    greet(dp, y_peer)
    greet(x_peer, mp)
    has_up, has_down = z < 3, z > 0

    @pl.when(has_up)
    def _():
        greet(dp + 2, mp)

    @pl.when(has_down)
    def _():
        greet(dp - 2, mp)

    @pl.when(has_up & has_down)
    def _():
        pl.semaphore_wait(barrier, 5)

    @pl.when(jnp.logical_not(has_up & has_down))
    def _():
        pl.semaphore_wait(barrier, 4)

    def token_copy(index, source, slot, mp_to):
        return pltpu.make_async_remote_copy(
            src_ref=source, dst_ref=tok.at[slot], send_sem=tsend.at[index],
            recv_sem=trecv.at[index], device_id={"dp": dp, "mp": mp_to}, device_id_type=MESH,
        )

    def weight_copy(way, z_from, source):
        slot = 2 * z_from + x
        dp_to = (dp + 2, dp - 2, x_peer)[way]
        return pltpu.make_async_remote_copy(
            src_ref=wbuf.at[slot] if source is None else source, dst_ref=wbuf.at[slot],
            send_sem=wsend.at[way, z_from], recv_sem=wrecv.at[slot],
            device_id={"dp": dp_to, "mp": mp}, device_id_type=MESH,
        )

    def weight_arrival(slot):
        pltpu.make_async_remote_copy(
            src_ref=wbuf.at[slot], dst_ref=wbuf.at[slot], send_sem=wsend.at[0, 0],
            recv_sem=wrecv.at[slot], device_id={"dp": x_peer, "mp": mp}, device_id_type=MESH,
        ).wait_recv()

    across = token_copy(0, tin, mp, y_peer)
    across.start()

    @pl.when(has_up)
    def _():
        weight_copy(0, z, win).start()

    @pl.when(has_down)
    def _():
        weight_copy(1, z, win).start()

    weight_copy(2, z, win).start()
    beside = token_copy(1, tin, mp, core_peer)
    beside.start()
    own = pltpu.make_async_copy(win, wbuf.at[dp], lsem)
    own.start()

    squares[...] = jnp.zeros_like(squares)

    def prepare(source, slot):
        @pl.loop(0, total // 96)
        def _(step):
            rows = pl.ds(pl.multiple_of(step * 96, 96), 96)
            values = source[rows, :].astype(jnp.float32)
            squares[rows, :] += jnp.sum(values * values, axis=-1, keepdims=True)
            scaled[slot, rows, :] = (values * gain[slot]).astype(jnp.bfloat16)

        pooled[slot] = jnp.dot(mask[...], source[...], preferred_element_type=jnp.float32)

    prepare(tin, mp)
    beside.wait_recv()
    prepare(tok.at[core_peer], core_peer)
    own.wait()

    def relay(k):
        @pl.when(z >= k)
        def _():
            weight_arrival(2 * (z - k) + x)

            @pl.when(has_up)
            def _():
                weight_copy(0, z - k, None).start()

            weight_copy(2, z - k, None).start()

        @pl.when(z + k <= 3)
        def _():
            weight_arrival(2 * (z + k) + x)

            @pl.when(has_down)
            def _():
                weight_copy(1, z + k, None).start()

            weight_copy(2, z + k, None).start()

    relay(1)
    relay(2)
    across.wait_recv()
    onward = token_copy(2, tok.at[y_peer], y_peer, core_peer)
    onward.start()
    relay(3)
    prepare(tok.at[y_peer], y_peer)
    onward.wait_recv()
    prepare(tok.at[far], far)

    width = 4 * tin.shape[1]
    columns = win.shape[1]

    def multiply(turn):
        block = (z, z + 1 - 2 * (z % 2), (z + 2) % 4, 3 - z)[turn]
        weight_arrival(2 * block + 1 - x)
        weights = wbuf.at[pl.ds(2 * block, 2)]

        @pl.loop(0, total // ROWS)
        def _(step):
            rows = pl.ds(pl.multiple_of(step * ROWS, ROWS), ROWS)
            product = jnp.dot(
                scaled[block, rows, :],
                weights[...].reshape(2 * win.shape[0], columns),
                preferred_element_type=jnp.float32,
            )
            if turn == 0:
                acc[rows, :] = product
            else:
                acc[rows, :] += product

    for turn in range(4):
        multiply(turn)

    @pl.loop(0, total // ROWS)
    def _(step):
        rows = pl.ds(pl.multiple_of(step * ROWS, ROWS), ROWS)
        scale = lax.rsqrt(squares[rows, :] * (1.0 / width) + 1e-06)
        for head in range(columns // HEAD_DIM):
            span = pl.ds(head * HEAD_DIM, HEAD_DIM)
            piece = acc[rows, span] * scale
            if head < columns // HEAD_DIM - 1:
                piece = piece * cosine[...] + pltpu.roll(piece, HEAD_DIM // 2, 1) * sine[...]
            qkv[rows, span] = piece.astype(jnp.bfloat16)

    across.wait_send()
    beside.wait_send()
    onward.wait_send()

    for z_from in range(4):
        @pl.when(has_up & (z >= z_from))
        def _():
            weight_copy(0, z_from, None).wait_send()

        @pl.when(has_down & (z <= z_from))
        def _():
            weight_copy(1, z_from, None).wait_send()

        weight_copy(2, z_from, None).wait_send()


def gather_project(tokens, norm_gain, w_query, w_keyval, lengths):
    dialogs, seq_len, part = tokens.shape
    total = dialogs * seq_len
    weights = jnp.concatenate([w_query, w_keyval.reshape(w_keyval.shape[0], -1)], axis=1)
    depth, columns = weights.shape
    positions = jnp.arange(seq_len)
    half = HEAD_DIM // 2
    freqs = rope_base ** (-jnp.arange(half, dtype=jnp.float32) * 2.0 / HEAD_DIM)
    angles = positions.astype(jnp.float32)[:, None] * freqs[None, :]
    cosine = jnp.cos(angles)
    sine = jnp.sin(angles)
    cosine = jnp.tile(jnp.concatenate([cosine, cosine], axis=1), (ROWS // seq_len, 1))
    sine = jnp.tile(jnp.concatenate([-sine, sine], axis=1), (ROWS // seq_len, 1))
    row = jnp.arange(total)[None, :]
    mine = jnp.arange(dialogs)[:, None]
    mask = ((row // seq_len == mine) & (row % seq_len < lengths[:, None])).astype(jnp.bfloat16)
    vmem = pl.BlockSpec(memory_space=pltpu.VMEM)
    qkv, pooled = pl.pallas_call(
        gather_project_kernel,
        out_shape=(
            jax.ShapeDtypeStruct((total, columns), jnp.bfloat16),
            jax.ShapeDtypeStruct((4, dialogs, part), jnp.float32),
        ),
        in_specs=[vmem] * 6,
        out_specs=(vmem, vmem),
        scratch_shapes=[
            pltpu.VMEM((4, total, part), jnp.bfloat16),
            pltpu.VMEM((8, depth, columns), jnp.bfloat16),
            pltpu.VMEM((4, total, part), jnp.bfloat16),
            pltpu.VMEM((total, columns), jnp.float32),
            pltpu.VMEM((total, 1), jnp.float32),
            pltpu.SemaphoreType.DMA((3,)),
            pltpu.SemaphoreType.DMA((3,)),
            pltpu.SemaphoreType.DMA((3, 4)),
            pltpu.SemaphoreType.DMA((8,)),
            pltpu.SemaphoreType.DMA,
        ],
        compiler_params=pltpu.CompilerParams(
            collective_id=0, has_side_effects=True, vmem_limit_bytes=58 * 1024 * 1024
        ),
    )(
        tokens.reshape(total, part), weights, norm_gain.reshape(4, 1, part), mask, cosine, sine
    )
    pooled_input = (pooled / lengths.astype(jnp.float32)[None, :, None]).transpose(1, 0, 2)
    queries = w_query.shape[1]
    shape = (dialogs, seq_len, -1, HEAD_DIM)
    return (
        qkv[:, :queries].reshape(shape),
        qkv[:, queries : queries + HEAD_DIM].reshape(shape),
        qkv[:, queries + HEAD_DIM :].reshape(shape),
        pooled_input.reshape(dialogs, 4 * part),
    )


def score_kernel(
    context, pooled, onehot, w_out, members, live, returned,
    own_rows, own_pooled, all_rows, all_pooled, exact, parts, others, sums, rows_in, joined,
    squares, replies, arrived,
    a_send, a_recv, c_send, c_recv, d_send, d_recv, f_send, f_recv,
):
    dp = lax.axis_index("dp")
    mp = lax.axis_index("mp")
    barrier = pltpu.get_barrier_semaphore()
    for i in range(8):
        for j in range(4):
            if i or j:
                pl.semaphore_signal(
                    barrier, inc=1, device_id={"dp": (dp + i) % 8, "mp": (mp + j) % 4},
                    device_id_type=MESH,
                )

    for o in range(8):
        own_pooled[o] = jnp.dot(
            onehot[...], pooled[o], preferred_element_type=jnp.float32
        ).astype(jnp.bfloat16)
    own_rows[...] = jnp.dot(
        onehot[...], context[...], preferred_element_type=jnp.float32
    ).astype(jnp.bfloat16)
    pl.semaphore_wait(barrier, 31)

    def remote(source, target, send, recv, dp_to, mp_to):
        return pltpu.make_async_remote_copy(
            src_ref=source, dst_ref=target, send_sem=send, recv_sem=recv,
            device_id={"dp": dp_to, "mp": mp_to}, device_id_type=MESH,
        )

    def rows_copy(i, slot):
        return remote(
            own_rows, all_rows.at[slot], a_send.at[0, i], a_recv.at[0, slot], (dp + i) % 8, mp
        )

    def pooled_copy(i, slot):
        to = (dp + i) % 8
        return remote(
            own_pooled.at[to], all_pooled.at[slot], a_send.at[1, i], a_recv.at[1, slot], to, mp
        )

    for i in range(1, 8):
        rows_copy(i, dp).start()
    for i in range(1, 8):
        pooled_copy(i, dp).start()
    all_rows[dp] = own_rows[...]
    all_pooled[dp] = own_pooled[dp]

    @pl.loop(0, members.shape[0] // 64)
    def _(step):
        rows = pl.ds(pl.multiple_of(step * 64, 64), 64)
        values = members[rows, :].astype(jnp.float32)
        squares[rows, :] = jnp.broadcast_to(
            jnp.sum(values * values, axis=-1, keepdims=True), (64, 128)
        )

    scale = live[...] * lax.rsqrt(squares[...].T[0:1, :] + 1e-06)
    row = lax.broadcasted_iota(jnp.int32, (256, 256), 0)
    column = lax.broadcasted_iota(jnp.int32, (256, 256), 1)
    target = ((row >> 2) & 7) * 32 + (row >> 5) * 4 + (row & 3)
    order = jnp.where(column == target, 1.0, 0.0).astype(jnp.bfloat16)
    for i in range(1, 8):
        rows_copy(i, (dp + i) % 8).wait_recv()
    sorted_rows = jnp.dot(
        order, all_rows[...].reshape(256, -1), preferred_element_type=jnp.float32
    ).astype(jnp.bfloat16)
    product = jnp.dot(sorted_rows, w_out[...], preferred_element_type=jnp.float32)
    parts[...] = product.astype(jnp.bfloat16).reshape(parts.shape)

    def part_copy(i, slot):
        to = (mp + i) % 4
        return remote(parts.at[to], others.at[slot], c_send.at[i], c_recv.at[slot], dp, to)

    for i in range(1, 4):
        part_copy(i, mp).start()
    for i in range(1, 8):
        pooled_copy(i, (dp + i) % 8).wait_recv()
    exact[...] = (
        product
        + jnp.dot(order, all_pooled[...].reshape(256, -1), preferred_element_type=jnp.float32)
    ).reshape(exact.shape)
    total = exact[mp]
    for i in range(1, 4):
        slot = (mp + i) % 4
        part_copy(i, slot).wait_recv()
        total = total + others[slot].astype(jnp.float32)
    sums[...] = total.astype(jnp.bfloat16).reshape(sums.shape)

    def sum_copy(j, i, slot):
        return remote(
            sums.at[j], rows_in.at[slot], d_send.at[j, i], d_recv.at[slot],
            2 * mp + j, (mp + i) % 4,
        )

    for j in range(2):
        mine = 2 * mp + j == dp

        @pl.when(jnp.logical_not(mine))
        def _():
            sum_copy(j, 0, dp).start()

        for i in range(1, 4):
            sum_copy(j, i, dp).start()

        @pl.when(mine)
        def _():
            rows_in[dp] = sums[j]

    for slot in range(8):
        @pl.when(jnp.logical_not((dp // 2 == mp) & (dp == slot)))
        def _():
            sum_copy(0, 0, slot).wait_recv()

    width = rows_in.shape[2]
    for slot in range(8):
        joined[:, slot * width : (slot + 1) * width] = rows_in[slot].astype(jnp.float32)
    embedding = joined[...]
    unit = embedding * lax.rsqrt(jnp.sum(embedding * embedding, axis=-1, keepdims=True) + 1e-06)
    dots = lax.dot_general(
        unit.astype(jnp.bfloat16), members[...], (((1,), (1,)), ((), ())),
        preferred_element_type=jnp.float32,
    )
    found = (dots * scale).astype(jnp.bfloat16)
    row = lax.broadcasted_iota(jnp.int32, (128, 32), 0)
    column = lax.broadcasted_iota(jnp.int32, (128, 32), 1)
    spread = jnp.where(((row & 15) < 4) & (column == (row >> 4) * 4 + (row & 15)), 1.0, 0.0)
    replies[...] = jnp.dot(
        spread.astype(jnp.bfloat16), found, preferred_element_type=jnp.float32
    ).astype(jnp.bfloat16).reshape(replies.shape)

    def reply_copy(i, slot):
        to = (dp + i) % 8
        return remote(replies.at[to], arrived.at[slot], f_send.at[i], f_recv.at[slot], to, mp)

    for i in range(1, 8):
        reply_copy(i, dp).start()
    arrived[dp] = replies[dp]
    for i in range(1, 8):
        reply_copy(i, (dp + i) % 8).wait_recv()
    returned[...] = arrived[...]

    for i in range(1, 8):
        rows_copy(i, dp).wait_send()
        pooled_copy(i, dp).wait_send()
        reply_copy(i, dp).wait_send()
    for i in range(1, 4):
        part_copy(i, mp).wait_send()
    for j in range(2):
        @pl.when(2 * mp + j != dp)
        def _():
            sum_copy(j, 0, dp).wait_send()

        for i in range(1, 4):
            sum_copy(j, i, dp).wait_send()


def score(pooled_context, pooled_input, w_out, members, onehot, live):
    dialogs, head_width = pooled_context.shape
    width = w_out.shape[1]
    member_count = members.shape[0]
    slots = onehot.reshape(-1, dialogs).astype(jnp.bfloat16)
    pooled = pooled_input.astype(jnp.bfloat16).reshape(dialogs, 8, width).transpose(1, 0, 2)
    vmem = pl.BlockSpec(memory_space=pltpu.VMEM)
    half, full = jnp.bfloat16, jnp.float32
    returned = pl.pallas_call(
        score_kernel,
        out_shape=jax.ShapeDtypeStruct((8, 16, member_count), half),
        in_specs=[vmem] * 6,
        out_specs=vmem,
        scratch_shapes=[
            pltpu.VMEM((32, head_width), half),
            pltpu.VMEM((8, 32, width), half),
            pltpu.VMEM((8, 32, head_width), half),
            pltpu.VMEM((8, 32, width), half),
            pltpu.VMEM((4, 64, width), full),
            pltpu.VMEM((4, 64, width), half),
            pltpu.VMEM((4, 64, width), half),
            pltpu.VMEM((2, 32, width), half),
            pltpu.VMEM((8, 32, width), half),
            pltpu.VMEM((32, 8 * width), full),
            pltpu.VMEM((member_count, 128), full),
            pltpu.VMEM((8, 16, member_count), half),
            pltpu.VMEM((8, 16, member_count), half),
            pltpu.SemaphoreType.DMA((2, 8)),
            pltpu.SemaphoreType.DMA((2, 8)),
            pltpu.SemaphoreType.DMA((4,)),
            pltpu.SemaphoreType.DMA((4,)),
            pltpu.SemaphoreType.DMA((2, 4)),
            pltpu.SemaphoreType.DMA((8,)),
            pltpu.SemaphoreType.DMA((8,)),
            pltpu.SemaphoreType.DMA((8,)),
        ],
        compiler_params=pltpu.CompilerParams(
            collective_id=1, has_side_effects=True, vmem_limit_bytes=32 * 1024 * 1024
        ),
    )(pooled_context, pooled, slots, w_out, members, live)
    return returned[:, : onehot.shape[1]]


def plain_project(tokens, norm_gain, w_query, w_keyval, lengths):
    gathered = lax.all_gather(tokens, "mp", axis=2, tiled=True)
    dialogs, seq_len, width = gathered.shape
    hidden = gathered.astype(jnp.float32)
    normed = (
        hidden * lax.rsqrt(jnp.mean(hidden * hidden, axis=-1, keepdims=True) + 1e-06) * norm_gain
    ).astype(jnp.bfloat16)
    normed_flat = normed.reshape(dialogs * seq_len, width)
    query_cols = w_query.shape[1]
    keyval_cols = w_keyval.shape[2]
    pieces = (
        lax.all_gather(w_query, "dp", axis=0, tiled=True),
        lax.all_gather(w_keyval, "dp", axis=0, tiled=True),
    )
    keyval_piece = pieces[1].reshape(pieces[1].shape[0], 2 * keyval_cols)
    query_sum = jnp.dot(normed_flat, pieces[0], preferred_element_type=jnp.float32)
    keyval_sum = jnp.dot(normed_flat, keyval_piece, preferred_element_type=jnp.float32)
    positions = jnp.arange(seq_len)
    local_heads = query_cols // HEAD_DIM
    local_kv = keyval_cols // HEAD_DIM
    query = jax.vmap(lambda block: rotate(block, positions))(
        query_sum.reshape(dialogs, seq_len, local_heads, HEAD_DIM)
    ).astype(jnp.bfloat16)
    keys = jax.vmap(lambda block: rotate(block, positions))(
        keyval_sum[:, :keyval_cols].reshape(dialogs, seq_len, local_kv, HEAD_DIM)
    ).astype(jnp.bfloat16)
    values = (
        keyval_sum[:, keyval_cols:]
        .reshape(dialogs, seq_len, local_kv, HEAD_DIM)
        .astype(jnp.bfloat16)
    )
    valid = (positions[None, :] < lengths[:, None]).astype(jnp.float32)
    pooled_input = (
        jnp.sum(hidden * valid[:, :, None], axis=1) / lengths.astype(jnp.float32)[:, None]
    )
    return query, keys, values, pooled_input


def plain_score(pooled_context, pooled_input, w_out, members, onehot, live):
    dialogs = pooled_context.shape[0]
    everyone = lax.all_gather(pooled_context, "dp", axis=0, tiled=True)
    slices = jnp.dot(everyone, w_out, preferred_element_type=jnp.float32).astype(jnp.bfloat16)
    slices = slices.reshape(-1, dialogs, w_out.shape[1])
    slices = lax.all_to_all(slices, "dp", split_axis=0, concat_axis=0, tiled=True)
    partial_out = slices.transpose(1, 0, 2).reshape(dialogs, -1)
    projected = lax.psum(partial_out, "mp").astype(jnp.float32)
    embedding = pooled_input + projected
    unit = embedding * lax.rsqrt(jnp.sum(embedding * embedding, axis=-1, keepdims=True) + 1e-06)
    unit = unit.astype(jnp.bfloat16)
    inverse_norm = lax.rsqrt(
        jnp.einsum("md,md->m", members, members, preferred_element_type=jnp.float32) + 1e-06
    )
    outgoing = jnp.einsum(
        "ocn,nd->ocd", onehot.astype(jnp.bfloat16), unit, preferred_element_type=jnp.float32
    ).astype(jnp.bfloat16)
    query_rows = lax.all_to_all(outgoing, "dp", split_axis=0, concat_axis=0, tiled=True)
    dots = lax.dot_general(
        query_rows,
        members,
        (((query_rows.ndim - 1,), (1,)), ((), ())),
        preferred_element_type=jnp.float32,
    )
    return lax.all_to_all(
        jnp.where(live[0] > 0, live[0] * dots * inverse_norm, 0.0).astype(jnp.bfloat16),
        "dp",
        split_axis=0,
        concat_axis=0,
        tiled=True,
    )


def local(
    tokens, norm_gain, w_query, w_keyval, w_out, residents, lengths, cluster, owner, counts, flags
):
    fast = lax.axis_size("dp") == 8 and lax.axis_size("mp") == 4
    if fast:
        project = gather_project
    else:
        project = plain_project
    query, keys, values, pooled_input = project(tokens, norm_gain, w_query, w_keyval, lengths)
    dialogs = query.shape[0]
    pooled_context = jax.vmap(attend)(query, keys, values, lengths).astype(jnp.bfloat16)
    my_index = lax.axis_index("dp")
    owner_count = lax.axis_size("dp")
    my_count = jnp.sum(jnp.where(owner == my_index, counts, 0))
    members = residents[0]
    member_count = members.shape[0]
    member_start = lax.axis_index("mp") * member_count
    live = jnp.where(member_start + jnp.arange(member_count) < my_count, logit_scale, 0.0)[None, :]
    table_size = owner.shape[0]
    cluster_ids = cluster[:, 0]
    destination = jnp.sum(
        jnp.where(jnp.arange(table_size)[None, :] == cluster_ids[:, None], owner[None, :], 0),
        axis=1,
    )
    capacity = max(1, -(-dialogs // owner_count))
    order = jnp.arange(dialogs)
    earlier = (destination[None, :] == destination[:, None]) & (order[None, :] < order[:, None])
    rank = jnp.sum(earlier.astype(jnp.int32), axis=1)
    onehot = (jnp.arange(owner_count)[:, None, None] == destination[None, None, :]) & (
        jnp.arange(capacity)[None, :, None] == rank[None, None, :]
    )
    if fast:
        assign = score
    else:
        assign = plain_score
    returned = assign(pooled_context, pooled_input, w_out, members, onehot, live)
    similarity = jnp.einsum(
        "ocn,ocm->nm", onehot.astype(jnp.bfloat16), returned, preferred_element_type=jnp.float32
    )
    return similarity * flags.astype(jnp.float32)[:, None]


def solution(mesh):
    in_specs = (
        P("dp", None, "mp"),
        P(),
        P("dp", "mp"),
        P("dp", None, "mp"),
        P("mp", "dp"),
        P("dp", "mp", None),
        P("dp"),
        P("dp", None),
        P(),
        P(),
        P("dp"),
    )
    out_specs = P("dp", "mp")
    return jax.shard_map(local, mesh=mesh, in_specs=in_specs, out_specs=out_specs, check_vma=False)
```

```python
import math

import jax
import jax.numpy as jnp
import numpy as np
from jax import lax
from jax.experimental import pallas as pl
from jax.experimental.pallas import tpu as pltpu
from jax.sharding import PartitionSpec as P

HEAD_DIM = 128


rope_base = 1000000.0
logit_scale = 100.0


def rotate(values, positions):
    half = values.shape[-1] // 2
    freqs = rope_base ** (-jnp.arange(half, dtype=jnp.float32) * 2.0 / values.shape[-1])
    angles = positions.astype(jnp.float32)[:, None] * freqs[None, :]
    cosine = jnp.cos(angles)[:, None, :]
    sine = jnp.sin(angles)[:, None, :]
    first = values[..., :half]
    second = values[..., half:]
    return jnp.concatenate(
        [first * cosine - second * sine, second * cosine + first * sine], axis=-1
    )


def attend(query, keys, values, length):
    seq_len = query.shape[0]
    kv_count = keys.shape[1]
    group = query.shape[1] // kv_count
    grouped = query.reshape(seq_len, kv_count, group, query.shape[-1])
    scores = jnp.einsum(
        "qkgd,pkd->kgqp", grouped, keys, preferred_element_type=jnp.float32
    ) / math.sqrt(query.shape[-1])
    row_pos = jnp.arange(seq_len)[:, None]
    col_pos = jnp.arange(seq_len)[None, :]
    allowed = (col_pos <= row_pos) & (col_pos < length)
    scores = jnp.where(allowed, scores, -1e30)
    highest = jnp.max(scores, axis=-1, keepdims=True)
    expanded = jnp.exp(scores - highest)
    weights = (expanded / jnp.sum(expanded, axis=-1, keepdims=True)).astype(jnp.bfloat16)
    context = jnp.einsum("kgqp,pkd->qkgd", weights, values, preferred_element_type=jnp.float32)
    valid = (jnp.arange(seq_len) < length).astype(jnp.float32)
    pooled = jnp.sum(context * valid[:, None, None, None], axis=0) / length.astype(jnp.float32)
    return pooled.reshape(-1)


MESH = pl.DeviceIdType.MESH
ROWS = 384
CHUNK = 4


def gather_project_kernel(
    tin, query_in, keyval_in, gain, lens, cosine, sine, place, context, pooled,
    tok, wbuf, scaled, acc, squares, mask, stash, heads,
    tsend, trecv, wsend, wrecv, hsend, hrecv, lsem,
):
    dp = lax.axis_index("dp")
    mp = lax.axis_index("mp")
    z, x = dp // 2, dp % 2
    core_peer = mp + 1 - 2 * (mp % 2)
    y_peer = (mp + 2) % 4
    far = (core_peer + 2) % 4
    x_peer = 2 * z + 1 - x
    total = tin.shape[0]
    depth, columns = wbuf.shape[1:]
    queries = query_in.shape[1]
    seq_len = total // lens.shape[0]
    own_query = pltpu.make_async_copy(query_in, wbuf.at[dp, :, pl.ds(0, queries)], lsem.at[0])
    own_keyval = pltpu.make_async_copy(
        keyval_in, wbuf.at[dp, :, pl.ds(queries, columns - queries)], lsem.at[1]
    )
    own_query.start()
    own_keyval.start()

    barrier = pltpu.get_barrier_semaphore()

    def greet(dp_to, mp_to):
        pl.semaphore_signal(
            barrier, inc=1, device_id={"dp": dp_to, "mp": mp_to}, device_id_type=MESH
        )

    greet(dp, core_peer)
    greet(dp, y_peer)
    greet(x_peer, mp)
    has_up, has_down = z < 3, z > 0

    @pl.when(has_up)
    def _():
        greet(dp + 2, mp)

    @pl.when(has_down)
    def _():
        greet(dp - 2, mp)

    @pl.when(has_up & has_down)
    def _():
        pl.semaphore_wait(barrier, 5)

    @pl.when(jnp.logical_not(has_up & has_down))
    def _():
        pl.semaphore_wait(barrier, 4)

    def token_copy(index, source, slot, mp_to):
        return pltpu.make_async_remote_copy(
            src_ref=source, dst_ref=tok.at[slot], send_sem=tsend.at[index],
            recv_sem=trecv.at[index], device_id={"dp": dp, "mp": mp_to}, device_id_type=MESH,
        )

    def weight_copy(way, z_from):
        slot = 2 * z_from + x
        dp_to = (dp + 2, dp - 2, x_peer)[way]
        return pltpu.make_async_remote_copy(
            src_ref=wbuf.at[slot], dst_ref=wbuf.at[slot],
            send_sem=wsend.at[way, z_from], recv_sem=wrecv.at[slot],
            device_id={"dp": dp_to, "mp": mp}, device_id_type=MESH,
        )

    def weight_arrival(slot):
        pltpu.make_async_remote_copy(
            src_ref=wbuf.at[slot], dst_ref=wbuf.at[slot], send_sem=wsend.at[0, 0],
            recv_sem=wrecv.at[slot], device_id={"dp": x_peer, "mp": mp}, device_id_type=MESH,
        ).wait_recv()

    pair = z + 1 - 2 * (z % 2)
    upper, lower = pl.ds(0, depth // 2), pl.ds(depth // 2, depth // 2)

    def pair_upper():
        slot = 2 * pair + x
        return pltpu.make_async_remote_copy(
            src_ref=wbuf.at[slot, upper], dst_ref=wbuf.at[slot, upper],
            send_sem=hsend.at[0], recv_sem=hrecv.at[0],
            device_id={"dp": x_peer, "mp": mp}, device_id_type=MESH,
        )

    def pair_lower():
        slot = 2 * z + 1 - x
        return pltpu.make_async_remote_copy(
            src_ref=wbuf.at[slot, lower], dst_ref=wbuf.at[slot, lower],
            send_sem=hsend.at[1], recv_sem=hrecv.at[1],
            device_id={"dp": 2 * pair + x, "mp": mp}, device_id_type=MESH,
        )

    def pair_arrival(index, rows):
        slot = 2 * pair + 1 - x
        pltpu.make_async_remote_copy(
            src_ref=wbuf.at[slot, rows], dst_ref=wbuf.at[slot, rows],
            send_sem=hsend.at[index], recv_sem=hrecv.at[index],
            device_id={"dp": x_peer, "mp": mp}, device_id_type=MESH,
        ).wait_recv()

    across = token_copy(0, tin, mp, y_peer)
    across.start()
    own_query.wait()
    own_keyval.wait()

    @pl.when(has_up)
    def _():
        weight_copy(0, z).start()

    @pl.when(has_down)
    def _():
        weight_copy(1, z).start()

    weight_copy(2, z).start()
    beside = token_copy(1, tin, mp, core_peer)
    beside.start()

    squares[...] = jnp.zeros_like(squares)
    index = lax.broadcasted_iota(jnp.int32, mask.shape, 1)
    first = lax.broadcasted_iota(jnp.int32, mask.shape, 0) * seq_len
    ahead = (index - first).astype(jnp.float32)
    mask[...] = jnp.where((ahead >= 0.0) & (ahead < lens[:, 0:1]), 1.0, 0.0).astype(mask.dtype)

    def prepare(source, slot):
        part = tin.shape[1]
        factor = gain[:, pl.ds(pl.multiple_of(slot * part, 128), part)]

        @pl.loop(0, total // 96)
        def _(step):
            rows = pl.ds(pl.multiple_of(step * 96, 96), 96)
            values = source[rows, :].astype(jnp.float32)
            squares[rows, :] += jnp.sum(values * values, axis=-1, keepdims=True)
            scaled[slot, rows, :] = (values * factor).astype(jnp.bfloat16)

        mean = jnp.dot(mask[...], source[...], preferred_element_type=jnp.float32) / lens[:, 0:1]
        pooled[2 * slot] = mean[:, : part // 2].astype(pooled.dtype)
        pooled[2 * slot + 1] = mean[:, part // 2 :].astype(pooled.dtype)

    prepare(tin, mp)
    beside.wait_recv()
    prepare(tok.at[core_peer], core_peer)

    def send_beside(k, z_from):
        if k > 1:
            weight_copy(2, z_from).start()
            return

        @pl.when(z_from == pair)
        def _():
            pair_upper().start()

        @pl.when(z_from != pair)
        def _():
            weight_copy(2, z_from).start()

    def relay(k):
        @pl.when(z >= k)
        def _():
            weight_arrival(2 * (z - k) + x)

            @pl.when(has_up)
            def _():
                weight_copy(0, z - k).start()

            send_beside(k, z - k)

        @pl.when(z + k <= 3)
        def _():
            weight_arrival(2 * (z + k) + x)

            @pl.when(has_down)
            def _():
                weight_copy(1, z + k).start()

            send_beside(k, z + k)

    relay(1)
    weight_arrival(2 * z + 1 - x)
    pair_lower().start()
    relay(2)
    across.wait_recv()
    onward = token_copy(2, tok.at[y_peer], y_peer, core_peer)
    onward.start()
    relay(3)
    prepare(tok.at[y_peer], y_peer)
    onward.wait_recv()
    prepare(tok.at[far], far)

    width = 4 * tin.shape[1]

    def multiply(turn):
        block = (z, pair, (z + 2) % 4, 3 - z)[turn]
        if turn == 1:
            pair_arrival(0, upper)
            pair_arrival(1, lower)
        elif turn > 1:
            weight_arrival(2 * block + 1 - x)
        weights = wbuf.at[pl.ds(2 * block, 2)]

        @pl.loop(0, total // ROWS)
        def _(step):
            rows = pl.ds(pl.multiple_of(step * ROWS, ROWS), ROWS)
            product = jnp.dot(
                scaled[block, rows, :],
                weights[...].reshape(2 * depth, columns),
                preferred_element_type=jnp.float32,
            )
            if turn == 0:
                acc[rows, :] = product
            else:
                acc[rows, :] += product

    for turn in range(4):
        multiply(turn)

    group = queries // HEAD_DIM
    lanes = (group + 1) * seq_len
    key_pos = lax.broadcasted_iota(jnp.int32, (seq_len, lanes), 0).astype(jnp.float32)
    query_pos = place[...]
    causal = key_pos <= query_pos
    head_start = lax.broadcasted_iota(jnp.int32, (8, lanes), 0) * seq_len
    offset = lax.broadcasted_iota(jnp.int32, (8, lanes), 1) - head_start
    same_head = (offset >= 0) & (offset < seq_len)
    block_rows = CHUNK * seq_len

    @pl.loop(0, total // block_rows)
    def _(step):
        rows = pl.ds(pl.multiple_of(step * block_rows, block_rows), block_rows)
        scale = lax.rsqrt(squares[rows, :] * (1.0 / width) + 1e-06)
        for head in range(columns // HEAD_DIM):
            span = pl.ds(head * HEAD_DIM, HEAD_DIM)
            piece = acc[rows, span] * scale
            if head < columns // HEAD_DIM - 1:
                piece = piece * cosine[...] + pltpu.roll(piece, HEAD_DIM // 2, 1) * sine[...]
            stash[:, span] = piece.astype(jnp.bfloat16)
        for item in range(CHUNK):
            here = slice(item * seq_len, (item + 1) * seq_len)
            stacked = jnp.concatenate(
                [stash[here, h * HEAD_DIM : (h + 1) * HEAD_DIM] for h in range(group + 1)], axis=0
            )
            keys = stash[here, queries : queries + HEAD_DIM]
            values = stash[here, queries + HEAD_DIM :]
            length = lens[pl.ds(step * CHUNK + item, 1), 0:1]
            scores = lax.dot_general(
                keys, stacked, (((1,), (1,)), ((), ())), preferred_element_type=jnp.float32
            ) * (1.0 / math.sqrt(HEAD_DIM))
            scores = jnp.where(causal & (key_pos < length), scores, -1e30)
            expanded = jnp.exp(scores - jnp.max(scores, axis=0, keepdims=True))
            weights = (expanded / jnp.sum(expanded, axis=0, keepdims=True)).astype(jnp.bfloat16)
            chosen = jnp.where(same_head & (query_pos < length), 1.0, 0.0).astype(jnp.bfloat16)
            sums = lax.dot_general(
                chosen, weights, (((1,), (1,)), ((), ())), preferred_element_type=jnp.float32
            )
            high = sums.astype(jnp.bfloat16).astype(jnp.float32)
            both = jnp.concatenate([high, sums - high], axis=0).astype(jnp.bfloat16)
            mixed = jnp.dot(both, values, preferred_element_type=jnp.float32)
            result = (mixed[:8] + mixed[8:]) / length
            heads[step * CHUNK + item] = result

    for h in range(group):
        context[:, h * HEAD_DIM : (h + 1) * HEAD_DIM] = heads[:, h, :]

    across.wait_send()
    beside.wait_send()
    onward.wait_send()

    for z_from in range(4):
        @pl.when(has_up & (z >= z_from))
        def _():
            weight_copy(0, z_from).wait_send()

        @pl.when(has_down & (z <= z_from))
        def _():
            weight_copy(1, z_from).wait_send()

        @pl.when(z_from != pair)
        def _():
            weight_copy(2, z_from).wait_send()

    pair_upper().wait_send()
    pair_lower().wait_send()


def gather_project(tokens, norm_gain, w_query, w_keyval, lengths):
    dialogs, seq_len, part = tokens.shape
    total = dialogs * seq_len
    depth, queries = w_query.shape
    keyval = w_keyval.reshape(depth, -1)
    columns = queries + keyval.shape[1]
    half = HEAD_DIM // 2
    freqs = rope_base ** (-np.arange(half, dtype=np.float64) * 2.0 / HEAD_DIM)
    angles = np.arange(seq_len, dtype=np.float64)[:, None] * freqs[None, :]
    cosine, sine = np.cos(angles), np.sin(angles)
    cosine = np.tile(np.concatenate([cosine, cosine], axis=1), (CHUNK, 1)).astype(np.float32)
    sine = np.tile(np.concatenate([-sine, sine], axis=1), (CHUNK, 1)).astype(np.float32)
    place = np.tile(np.arange(seq_len), queries // HEAD_DIM + 1).astype(np.float32)[None, :]
    lens = jnp.broadcast_to(lengths.astype(jnp.float32)[:, None], (dialogs, 128))
    vmem = pl.BlockSpec(memory_space=pltpu.VMEM)
    return pl.pallas_call(
        gather_project_kernel,
        out_shape=(
            jax.ShapeDtypeStruct((dialogs, queries), jnp.float32),
            jax.ShapeDtypeStruct((8, dialogs, part // 2), jnp.bfloat16),
        ),
        in_specs=[vmem] * 8,
        out_specs=(vmem, vmem),
        scratch_shapes=[
            pltpu.VMEM((4, total, part), jnp.bfloat16),
            pltpu.VMEM((8, depth, columns), jnp.bfloat16),
            pltpu.VMEM((4, total, part), jnp.bfloat16),
            pltpu.VMEM((total, columns), jnp.float32),
            pltpu.VMEM((total, 1), jnp.float32),
            pltpu.VMEM((dialogs, total), jnp.bfloat16),
            pltpu.VMEM((CHUNK * seq_len, columns), jnp.bfloat16),
            pltpu.VMEM((dialogs, 8, HEAD_DIM), jnp.float32),
            pltpu.SemaphoreType.DMA((3,)),
            pltpu.SemaphoreType.DMA((3,)),
            pltpu.SemaphoreType.DMA((3, 4)),
            pltpu.SemaphoreType.DMA((8,)),
            pltpu.SemaphoreType.DMA((2,)),
            pltpu.SemaphoreType.DMA((2,)),
            pltpu.SemaphoreType.DMA((2,)),
        ],
        compiler_params=pltpu.CompilerParams(
            collective_id=0, has_side_effects=True, vmem_limit_bytes=58 * 1024 * 1024
        ),
    )(
        tokens.reshape(total, part), w_query, keyval, norm_gain.reshape(1, -1), lens, cosine, sine,
        place,
    )


def score_kernel(
    context, pooled, onehot, w_out, members_in, live, returned, members,
    own_rows, own_pooled, all_rows, all_pooled, exact, parts, others, sums, rows_in, joined,
    squares, replies, arrived,
    a_send, a_recv, c_send, c_recv, d_send, d_recv, f_send, f_recv, l_sem,
):
    dp = lax.axis_index("dp")
    mp = lax.axis_index("mp")
    load = pltpu.make_async_copy(members_in, members, l_sem)
    load.start()
    barrier = pltpu.get_barrier_semaphore()
    for i in range(8):
        for j in range(4):
            if i or j:
                pl.semaphore_signal(
                    barrier, inc=1, device_id={"dp": (dp + i) % 8, "mp": (mp + j) % 4},
                    device_id_type=MESH,
                )

    for o in range(8):
        own_pooled[o] = jnp.dot(
            onehot[...], pooled[o], preferred_element_type=jnp.float32
        ).astype(jnp.bfloat16)
    own_rows[...] = jnp.dot(
        onehot[...], context[...].astype(jnp.bfloat16), preferred_element_type=jnp.float32
    ).astype(jnp.bfloat16)
    pl.semaphore_wait(barrier, 31)

    def remote(source, target, send, recv, dp_to, mp_to):
        return pltpu.make_async_remote_copy(
            src_ref=source, dst_ref=target, send_sem=send, recv_sem=recv,
            device_id={"dp": dp_to, "mp": mp_to}, device_id_type=MESH,
        )

    def rows_copy(i, slot):
        return remote(
            own_rows, all_rows.at[slot], a_send.at[0, i], a_recv.at[0, slot], (dp + i) % 8, mp
        )

    def pooled_copy(i, slot):
        to = (dp + i) % 8
        return remote(
            own_pooled.at[to], all_pooled.at[slot], a_send.at[1, i], a_recv.at[1, slot], to, mp
        )

    for i in range(1, 8):
        rows_copy(i, dp).start()
    for i in range(1, 8):
        pooled_copy(i, dp).start()
    all_rows[dp] = own_rows[...]
    all_pooled[dp] = own_pooled[dp]

    load.wait()

    @pl.loop(0, members.shape[0] // 64)
    def _(step):
        rows = pl.ds(pl.multiple_of(step * 64, 64), 64)
        values = members[rows, :].astype(jnp.float32)
        squares[rows, :] = jnp.broadcast_to(
            jnp.sum(values * values, axis=-1, keepdims=True), (64, 128)
        )

    scale = live[...] * lax.rsqrt(squares[...].T[0:1, :] + 1e-06)
    row = lax.broadcasted_iota(jnp.int32, (256, 256), 0)
    column = lax.broadcasted_iota(jnp.int32, (256, 256), 1)
    target = ((row >> 2) & 7) * 32 + (row >> 5) * 4 + (row & 3)
    order = jnp.where(column == target, 1.0, 0.0).astype(jnp.bfloat16)
    for i in range(1, 8):
        rows_copy(i, (dp + i) % 8).wait_recv()
    sorted_rows = jnp.dot(
        order, all_rows[...].reshape(256, -1), preferred_element_type=jnp.float32
    ).astype(jnp.bfloat16)
    product = jnp.dot(sorted_rows, w_out[...], preferred_element_type=jnp.float32)
    parts[...] = product.astype(jnp.bfloat16).reshape(parts.shape)

    def part_copy(i, slot):
        to = (mp + i) % 4
        return remote(parts.at[to], others.at[slot], c_send.at[i], c_recv.at[slot], dp, to)

    for i in range(1, 4):
        part_copy(i, mp).start()
    for i in range(1, 8):
        pooled_copy(i, (dp + i) % 8).wait_recv()
    exact[...] = (
        product
        + jnp.dot(order, all_pooled[...].reshape(256, -1), preferred_element_type=jnp.float32)
    ).reshape(exact.shape)
    total = exact[mp]
    for i in range(1, 4):
        slot = (mp + i) % 4
        part_copy(i, slot).wait_recv()
        total = total + others[slot].astype(jnp.float32)
    sums[...] = total.astype(jnp.bfloat16).reshape(sums.shape)

    def sum_copy(j, i, slot):
        return remote(
            sums.at[j], rows_in.at[slot], d_send.at[j, i], d_recv.at[slot],
            2 * mp + j, (mp + i) % 4,
        )

    for j in range(2):
        mine = 2 * mp + j == dp

        @pl.when(jnp.logical_not(mine))
        def _():
            sum_copy(j, 0, dp).start()

        for i in range(1, 4):
            sum_copy(j, i, dp).start()

        @pl.when(mine)
        def _():
            rows_in[dp] = sums[j]

    for slot in range(8):
        @pl.when(jnp.logical_not((dp // 2 == mp) & (dp == slot)))
        def _():
            sum_copy(0, 0, slot).wait_recv()

    width = rows_in.shape[2]
    for slot in range(8):
        joined[:, slot * width : (slot + 1) * width] = rows_in[slot].astype(jnp.float32)
    embedding = joined[...]
    unit = embedding * lax.rsqrt(jnp.sum(embedding * embedding, axis=-1, keepdims=True) + 1e-06)
    dots = lax.dot_general(
        unit.astype(jnp.bfloat16), members[...], (((1,), (1,)), ((), ())),
        preferred_element_type=jnp.float32,
    )
    found = (dots * scale).astype(jnp.bfloat16)
    row = lax.broadcasted_iota(jnp.int32, (128, 32), 0)
    column = lax.broadcasted_iota(jnp.int32, (128, 32), 1)
    spread = jnp.where(((row & 15) < 4) & (column == (row >> 4) * 4 + (row & 15)), 1.0, 0.0)
    replies[...] = jnp.dot(
        spread.astype(jnp.bfloat16), found, preferred_element_type=jnp.float32
    ).astype(jnp.bfloat16).reshape(replies.shape)

    def reply_copy(i, slot):
        to = (dp + i) % 8
        return remote(replies.at[to], arrived.at[slot], f_send.at[i], f_recv.at[slot], to, mp)

    for i in range(1, 8):
        reply_copy(i, dp).start()
    arrived[dp] = replies[dp]
    for i in range(1, 8):
        reply_copy(i, (dp + i) % 8).wait_recv()
    returned[...] = arrived[...]

    for i in range(1, 8):
        rows_copy(i, dp).wait_send()
        pooled_copy(i, dp).wait_send()
        reply_copy(i, dp).wait_send()
    for i in range(1, 4):
        part_copy(i, mp).wait_send()
    for j in range(2):
        @pl.when(2 * mp + j != dp)
        def _():
            sum_copy(j, 0, dp).wait_send()

        for i in range(1, 4):
            sum_copy(j, i, dp).wait_send()


def score(pooled_context, pooled_input, w_out, members, onehot, live):
    dialogs, head_width = pooled_context.shape
    width = w_out.shape[1]
    member_count = members.shape[0]
    slots = onehot.reshape(-1, dialogs).astype(jnp.bfloat16)
    vmem = pl.BlockSpec(memory_space=pltpu.VMEM)
    half, full = jnp.bfloat16, jnp.float32
    returned = pl.pallas_call(
        score_kernel,
        out_shape=jax.ShapeDtypeStruct((8, 16, member_count), half),
        in_specs=[vmem] * 4 + [pl.BlockSpec(memory_space=pl.ANY), vmem],
        out_specs=vmem,
        scratch_shapes=[
            pltpu.VMEM(members.shape, half),
            pltpu.VMEM((32, head_width), half),
            pltpu.VMEM((8, 32, width), half),
            pltpu.VMEM((8, 32, head_width), half),
            pltpu.VMEM((8, 32, width), half),
            pltpu.VMEM((4, 64, width), full),
            pltpu.VMEM((4, 64, width), half),
            pltpu.VMEM((4, 64, width), half),
            pltpu.VMEM((2, 32, width), half),
            pltpu.VMEM((8, 32, width), half),
            pltpu.VMEM((32, 8 * width), full),
            pltpu.VMEM((member_count, 128), full),
            pltpu.VMEM((8, 16, member_count), half),
            pltpu.VMEM((8, 16, member_count), half),
            pltpu.SemaphoreType.DMA((2, 8)),
            pltpu.SemaphoreType.DMA((2, 8)),
            pltpu.SemaphoreType.DMA((4,)),
            pltpu.SemaphoreType.DMA((4,)),
            pltpu.SemaphoreType.DMA((2, 4)),
            pltpu.SemaphoreType.DMA((8,)),
            pltpu.SemaphoreType.DMA((8,)),
            pltpu.SemaphoreType.DMA((8,)),
            pltpu.SemaphoreType.DMA,
        ],
        compiler_params=pltpu.CompilerParams(
            collective_id=1, has_side_effects=True, vmem_limit_bytes=32 * 1024 * 1024
        ),
    )(pooled_context, pooled_input, slots, w_out, members, live)
    return returned[:, : onehot.shape[1]]


def plain_project(tokens, norm_gain, w_query, w_keyval, lengths):
    gathered = lax.all_gather(tokens, "mp", axis=2, tiled=True)
    dialogs, seq_len, width = gathered.shape
    hidden = gathered.astype(jnp.float32)
    normed = (
        hidden * lax.rsqrt(jnp.mean(hidden * hidden, axis=-1, keepdims=True) + 1e-06) * norm_gain
    ).astype(jnp.bfloat16)
    normed_flat = normed.reshape(dialogs * seq_len, width)
    query_cols = w_query.shape[1]
    keyval_cols = w_keyval.shape[2]
    pieces = (
        lax.all_gather(w_query, "dp", axis=0, tiled=True),
        lax.all_gather(w_keyval, "dp", axis=0, tiled=True),
    )
    keyval_piece = pieces[1].reshape(pieces[1].shape[0], 2 * keyval_cols)
    query_sum = jnp.dot(normed_flat, pieces[0], preferred_element_type=jnp.float32)
    keyval_sum = jnp.dot(normed_flat, keyval_piece, preferred_element_type=jnp.float32)
    positions = jnp.arange(seq_len)
    local_heads = query_cols // HEAD_DIM
    local_kv = keyval_cols // HEAD_DIM
    query = jax.vmap(lambda block: rotate(block, positions))(
        query_sum.reshape(dialogs, seq_len, local_heads, HEAD_DIM)
    ).astype(jnp.bfloat16)
    keys = jax.vmap(lambda block: rotate(block, positions))(
        keyval_sum[:, :keyval_cols].reshape(dialogs, seq_len, local_kv, HEAD_DIM)
    ).astype(jnp.bfloat16)
    values = (
        keyval_sum[:, keyval_cols:]
        .reshape(dialogs, seq_len, local_kv, HEAD_DIM)
        .astype(jnp.bfloat16)
    )
    valid = (positions[None, :] < lengths[:, None]).astype(jnp.float32)
    pooled_input = (
        jnp.sum(hidden * valid[:, :, None], axis=1) / lengths.astype(jnp.float32)[:, None]
    )
    pooled_context = jax.vmap(attend)(query, keys, values, lengths).astype(jnp.bfloat16)
    return pooled_context, pooled_input


def plain_score(pooled_context, pooled_input, w_out, members, onehot, live):
    dialogs = pooled_context.shape[0]
    everyone = lax.all_gather(pooled_context, "dp", axis=0, tiled=True)
    slices = jnp.dot(everyone, w_out, preferred_element_type=jnp.float32).astype(jnp.bfloat16)
    slices = slices.reshape(-1, dialogs, w_out.shape[1])
    slices = lax.all_to_all(slices, "dp", split_axis=0, concat_axis=0, tiled=True)
    partial_out = slices.transpose(1, 0, 2).reshape(dialogs, -1)
    projected = lax.psum(partial_out, "mp").astype(jnp.float32)
    embedding = pooled_input + projected
    unit = embedding * lax.rsqrt(jnp.sum(embedding * embedding, axis=-1, keepdims=True) + 1e-06)
    unit = unit.astype(jnp.bfloat16)
    inverse_norm = lax.rsqrt(
        jnp.einsum("md,md->m", members, members, preferred_element_type=jnp.float32) + 1e-06
    )
    outgoing = jnp.einsum(
        "ocn,nd->ocd", onehot.astype(jnp.bfloat16), unit, preferred_element_type=jnp.float32
    ).astype(jnp.bfloat16)
    query_rows = lax.all_to_all(outgoing, "dp", split_axis=0, concat_axis=0, tiled=True)
    dots = lax.dot_general(
        query_rows,
        members,
        (((query_rows.ndim - 1,), (1,)), ((), ())),
        preferred_element_type=jnp.float32,
    )
    return lax.all_to_all(
        jnp.where(live[0] > 0, live[0] * dots * inverse_norm, 0.0).astype(jnp.bfloat16),
        "dp",
        split_axis=0,
        concat_axis=0,
        tiled=True,
    )


def local(
    tokens, norm_gain, w_query, w_keyval, w_out, residents, lengths, cluster, owner, counts, flags
):
    fast = lax.axis_size("dp") == 8 and lax.axis_size("mp") == 4
    if fast:
        project = gather_project
    else:
        project = plain_project
    pooled_context, pooled_input = project(tokens, norm_gain, w_query, w_keyval, lengths)
    dialogs = tokens.shape[0]
    my_index = lax.axis_index("dp")
    owner_count = lax.axis_size("dp")
    my_count = jnp.sum(jnp.where(owner == my_index, counts, 0))
    members = residents[0]
    member_count = members.shape[0]
    member_start = lax.axis_index("mp") * member_count
    live = jnp.where(member_start + jnp.arange(member_count) < my_count, logit_scale, 0.0)[None, :]
    table_size = owner.shape[0]
    cluster_ids = cluster[:, 0]
    destination = jnp.sum(
        jnp.where(jnp.arange(table_size)[None, :] == cluster_ids[:, None], owner[None, :], 0),
        axis=1,
    )
    capacity = max(1, -(-dialogs // owner_count))
    order = jnp.arange(dialogs)
    earlier = (destination[None, :] == destination[:, None]) & (order[None, :] < order[:, None])
    rank = jnp.sum(earlier.astype(jnp.int32), axis=1)
    onehot = (jnp.arange(owner_count)[:, None, None] == destination[None, None, :]) & (
        jnp.arange(capacity)[None, :, None] == rank[None, None, :]
    )
    if fast:
        assign = score
    else:
        assign = plain_score
    returned = assign(pooled_context, pooled_input, w_out, members, onehot, live)
    similarity = jnp.einsum(
        "ocn,ocm->nm", onehot.astype(jnp.bfloat16), returned, preferred_element_type=jnp.float32
    )
    return similarity * flags.astype(jnp.float32)[:, None]


def solution(mesh):
    in_specs = (
        P("dp", None, "mp"),
        P(),
        P("dp", "mp"),
        P("dp", None, "mp"),
        P("mp", "dp"),
        P("dp", "mp"),
        P("dp"),
        P("dp"),
        P(),
        P(),
        P("dp"),
    )
    out_specs = P("dp", "mp")
    return jax.shard_map(local, mesh=mesh, in_specs=in_specs, out_specs=out_specs, check_vma=False)
```

```python
import math

import jax
import jax.numpy as jnp
import numpy as np
from jax import lax
from jax.experimental import pallas as pl
from jax.experimental.pallas import tpu as pltpu
from jax.sharding import PartitionSpec as P

HEAD_DIM = 128


rope_base = 1000000.0
logit_scale = 100.0


def rotate(values, positions):
    half = values.shape[-1] // 2
    freqs = rope_base ** (-jnp.arange(half, dtype=jnp.float32) * 2.0 / values.shape[-1])
    angles = positions.astype(jnp.float32)[:, None] * freqs[None, :]
    cosine = jnp.cos(angles)[:, None, :]
    sine = jnp.sin(angles)[:, None, :]
    first = values[..., :half]
    second = values[..., half:]
    return jnp.concatenate(
        [first * cosine - second * sine, second * cosine + first * sine], axis=-1
    )


def attend(query, keys, values, length):
    seq_len = query.shape[0]
    kv_count = keys.shape[1]
    group = query.shape[1] // kv_count
    grouped = query.reshape(seq_len, kv_count, group, query.shape[-1])
    scores = jnp.einsum(
        "qkgd,pkd->kgqp", grouped, keys, preferred_element_type=jnp.float32
    ) / math.sqrt(query.shape[-1])
    row_pos = jnp.arange(seq_len)[:, None]
    col_pos = jnp.arange(seq_len)[None, :]
    allowed = (col_pos <= row_pos) & (col_pos < length)
    scores = jnp.where(allowed, scores, -1e30)
    highest = jnp.max(scores, axis=-1, keepdims=True)
    expanded = jnp.exp(scores - highest)
    weights = (expanded / jnp.sum(expanded, axis=-1, keepdims=True)).astype(jnp.bfloat16)
    context = jnp.einsum("kgqp,pkd->qkgd", weights, values, preferred_element_type=jnp.float32)
    valid = (jnp.arange(seq_len) < length).astype(jnp.float32)
    pooled = jnp.sum(context * valid[:, None, None, None], axis=0) / length.astype(jnp.float32)
    return pooled.reshape(-1)


MESH = pl.DeviceIdType.MESH
ROWS = 384
CHUNK = 4


def gather_project_kernel(
    tin, query_in, keyval_in, gain, lens, cosine, sine, place, context, pooled,
    tok, wbuf, scaled, acc, squares, mask, stash, heads,
    tsend, trecv, wsend, wrecv, lsem,
):
    dp = lax.axis_index("dp")
    mp = lax.axis_index("mp")
    z, x = dp // 2, dp % 2
    core_peer = mp + 1 - 2 * (mp % 2)
    y_peer = (mp + 2) % 4
    far = (core_peer + 2) % 4
    x_peer = 2 * z + 1 - x
    total = tin.shape[0]
    depth, columns = wbuf.shape[1:]
    queries = query_in.shape[1]
    seq_len = total // lens.shape[0]
    own_query = pltpu.make_async_copy(query_in, wbuf.at[dp, :, pl.ds(0, queries)], lsem.at[0])
    own_keyval = pltpu.make_async_copy(
        keyval_in, wbuf.at[dp, :, pl.ds(queries, columns - queries)], lsem.at[1]
    )
    own_query.start()
    own_keyval.start()

    barrier = pltpu.get_barrier_semaphore()

    def greet(dp_to, mp_to):
        pl.semaphore_signal(
            barrier, inc=1, device_id={"dp": dp_to, "mp": mp_to}, device_id_type=MESH
        )

    greet(dp, core_peer)
    greet(dp, y_peer)
    greet(x_peer, mp)
    has_up, has_down = z < 3, z > 0

    @pl.when(has_up)
    def _():
        greet(dp + 2, mp)

    @pl.when(has_down)
    def _():
        greet(dp - 2, mp)

    @pl.when(has_up & has_down)
    def _():
        pl.semaphore_wait(barrier, 5)

    @pl.when(jnp.logical_not(has_up & has_down))
    def _():
        pl.semaphore_wait(barrier, 4)

    def token_copy(index, source, slot, mp_to):
        return pltpu.make_async_remote_copy(
            src_ref=source, dst_ref=tok.at[slot], send_sem=tsend.at[index],
            recv_sem=trecv.at[index], device_id={"dp": dp, "mp": mp_to}, device_id_type=MESH,
        )

    def weight_copy(way, z_from):
        slot = 2 * z_from + x
        dp_to = (dp + 2, dp - 2, x_peer)[way]
        return pltpu.make_async_remote_copy(
            src_ref=wbuf.at[slot], dst_ref=wbuf.at[slot],
            send_sem=wsend.at[way, z_from], recv_sem=wrecv.at[slot],
            device_id={"dp": dp_to, "mp": mp}, device_id_type=MESH,
        )

    def weight_arrival(slot):
        pltpu.make_async_remote_copy(
            src_ref=wbuf.at[slot], dst_ref=wbuf.at[slot], send_sem=wsend.at[0, 0],
            recv_sem=wrecv.at[slot], device_id={"dp": x_peer, "mp": mp}, device_id_type=MESH,
        ).wait_recv()

    pair = z + 1 - 2 * (z % 2)

    across = token_copy(0, tin, mp, y_peer)
    across.start()
    own_query.wait()
    own_keyval.wait()

    @pl.when(has_up)
    def _():
        weight_copy(0, z).start()

    @pl.when(has_down)
    def _():
        weight_copy(1, z).start()

    weight_copy(2, z).start()
    beside = token_copy(1, tin, mp, core_peer)
    beside.start()

    squares[...] = jnp.zeros_like(squares)
    index = lax.broadcasted_iota(jnp.int32, mask.shape, 1)
    first = lax.broadcasted_iota(jnp.int32, mask.shape, 0) * seq_len
    ahead = (index - first).astype(jnp.float32)
    mask[...] = jnp.where((ahead >= 0.0) & (ahead < lens[:, 0:1]), 1.0, 0.0).astype(mask.dtype)

    def prepare(source, slot):
        part = tin.shape[1]
        factor = gain[:, pl.ds(pl.multiple_of(slot * part, 128), part)]

        @pl.loop(0, total // 96)
        def _(step):
            rows = pl.ds(pl.multiple_of(step * 96, 96), 96)
            values = source[rows, :].astype(jnp.float32)
            squares[rows, :] += jnp.sum(values * values, axis=-1, keepdims=True)
            scaled[slot, rows, :] = (values * factor).astype(jnp.bfloat16)

        mean = jnp.dot(mask[...], source[...], preferred_element_type=jnp.float32) / lens[:, 0:1]
        pooled[2 * slot] = mean[:, : part // 2].astype(pooled.dtype)
        pooled[2 * slot + 1] = mean[:, part // 2 :].astype(pooled.dtype)

    prepare(tin, mp)
    beside.wait_recv()
    prepare(tok.at[core_peer], core_peer)

    def relay(k):
        @pl.when(z >= k)
        def _():
            weight_arrival(2 * (z - k) + x)

            @pl.when(has_up)
            def _():
                weight_copy(0, z - k).start()

            weight_copy(2, z - k).start()

        @pl.when(z + k <= 3)
        def _():
            weight_arrival(2 * (z + k) + x)

            @pl.when(has_down)
            def _():
                weight_copy(1, z + k).start()

            weight_copy(2, z + k).start()

    relay(1)
    relay(2)
    across.wait_recv()
    onward = token_copy(2, tok.at[y_peer], y_peer, core_peer)
    onward.start()
    relay(3)
    prepare(tok.at[y_peer], y_peer)
    onward.wait_recv()
    prepare(tok.at[far], far)

    width = 4 * tin.shape[1]

    def multiply(turn):
        block = (z, pair, (z + 2) % 4, 3 - z)[turn]
        weight_arrival(2 * block + 1 - x)
        weights = wbuf.at[pl.ds(2 * block, 2)]

        @pl.loop(0, total // ROWS)
        def _(step):
            rows = pl.ds(pl.multiple_of(step * ROWS, ROWS), ROWS)
            product = jnp.dot(
                scaled[block, rows, :],
                weights[...].reshape(2 * depth, columns),
                preferred_element_type=jnp.float32,
            )
            if turn == 0:
                acc[rows, :] = product
            else:
                acc[rows, :] += product

    for turn in range(4):
        multiply(turn)

    group = queries // HEAD_DIM
    lanes = (group + 1) * seq_len
    key_pos = lax.broadcasted_iota(jnp.int32, (seq_len, lanes), 0).astype(jnp.float32)
    query_pos = place[...]
    causal = key_pos <= query_pos
    head_start = lax.broadcasted_iota(jnp.int32, (8, lanes), 0) * seq_len
    offset = lax.broadcasted_iota(jnp.int32, (8, lanes), 1) - head_start
    same_head = (offset >= 0) & (offset < seq_len)
    block_rows = CHUNK * seq_len

    @pl.loop(0, total // block_rows)
    def _(step):
        rows = pl.ds(pl.multiple_of(step * block_rows, block_rows), block_rows)
        scale = lax.rsqrt(squares[rows, :] * (1.0 / width) + 1e-06)
        for head in range(columns // HEAD_DIM):
            span = pl.ds(head * HEAD_DIM, HEAD_DIM)
            piece = acc[rows, span] * scale
            if head < columns // HEAD_DIM - 1:
                piece = piece * cosine[...] + pltpu.roll(piece, HEAD_DIM // 2, 1) * sine[...]
            stash[:, span] = piece.astype(jnp.bfloat16)
        for item in range(CHUNK):
            here = slice(item * seq_len, (item + 1) * seq_len)
            stacked = jnp.concatenate(
                [stash[here, h * HEAD_DIM : (h + 1) * HEAD_DIM] for h in range(group + 1)], axis=0
            )
            keys = stash[here, queries : queries + HEAD_DIM]
            values = stash[here, queries + HEAD_DIM :]
            length = lens[pl.ds(step * CHUNK + item, 1), 0:1]
            scores = lax.dot_general(
                keys, stacked, (((1,), (1,)), ((), ())), preferred_element_type=jnp.float32
            ) * (1.0 / math.sqrt(HEAD_DIM))
            scores = jnp.where(causal & (key_pos < length), scores, -1e30)
            expanded = jnp.exp(scores - jnp.max(scores, axis=0, keepdims=True))
            weights = (expanded / jnp.sum(expanded, axis=0, keepdims=True)).astype(jnp.bfloat16)
            chosen = jnp.where(same_head & (query_pos < length), 1.0, 0.0).astype(jnp.bfloat16)
            sums = lax.dot_general(
                chosen, weights, (((1,), (1,)), ((), ())), preferred_element_type=jnp.float32
            )
            high = sums.astype(jnp.bfloat16).astype(jnp.float32)
            both = jnp.concatenate([high, sums - high], axis=0).astype(jnp.bfloat16)
            mixed = jnp.dot(both, values, preferred_element_type=jnp.float32)
            result = (mixed[:8] + mixed[8:]) / length
            heads[step * CHUNK + item] = result

    for h in range(group):
        context[:, h * HEAD_DIM : (h + 1) * HEAD_DIM] = heads[:, h, :]

    across.wait_send()
    beside.wait_send()
    onward.wait_send()

    for z_from in range(4):
        @pl.when(has_up & (z >= z_from))
        def _():
            weight_copy(0, z_from).wait_send()

        @pl.when(has_down & (z <= z_from))
        def _():
            weight_copy(1, z_from).wait_send()

        weight_copy(2, z_from).wait_send()


def gather_project(tokens, norm_gain, w_query, w_keyval, lengths):
    dialogs, seq_len, part = tokens.shape
    total = dialogs * seq_len
    depth, queries = w_query.shape
    keyval = w_keyval.reshape(depth, -1)
    columns = queries + keyval.shape[1]
    half = HEAD_DIM // 2
    freqs = rope_base ** (-np.arange(half, dtype=np.float64) * 2.0 / HEAD_DIM)
    angles = np.arange(seq_len, dtype=np.float64)[:, None] * freqs[None, :]
    cosine, sine = np.cos(angles), np.sin(angles)
    cosine = np.tile(np.concatenate([cosine, cosine], axis=1), (CHUNK, 1)).astype(np.float32)
    sine = np.tile(np.concatenate([-sine, sine], axis=1), (CHUNK, 1)).astype(np.float32)
    place = np.tile(np.arange(seq_len), queries // HEAD_DIM + 1).astype(np.float32)[None, :]
    lens = jnp.broadcast_to(lengths.astype(jnp.float32)[:, None], (dialogs, 128))
    vmem = pl.BlockSpec(memory_space=pltpu.VMEM)
    return pl.pallas_call(
        gather_project_kernel,
        out_shape=(
            jax.ShapeDtypeStruct((dialogs, queries), jnp.float32),
            jax.ShapeDtypeStruct((8, dialogs, part // 2), jnp.bfloat16),
        ),
        in_specs=[vmem] * 8,
        out_specs=(vmem, vmem),
        scratch_shapes=[
            pltpu.VMEM((4, total, part), jnp.bfloat16),
            pltpu.VMEM((8, depth, columns), jnp.bfloat16),
            pltpu.VMEM((4, total, part), jnp.bfloat16),
            pltpu.VMEM((total, columns), jnp.float32),
            pltpu.VMEM((total, 1), jnp.float32),
            pltpu.VMEM((dialogs, total), jnp.bfloat16),
            pltpu.VMEM((CHUNK * seq_len, columns), jnp.bfloat16),
            pltpu.VMEM((dialogs, 8, HEAD_DIM), jnp.float32),
            pltpu.SemaphoreType.DMA((3,)),
            pltpu.SemaphoreType.DMA((3,)),
            pltpu.SemaphoreType.DMA((3, 4)),
            pltpu.SemaphoreType.DMA((8,)),
            pltpu.SemaphoreType.DMA((2,)),
        ],
        compiler_params=pltpu.CompilerParams(
            collective_id=0, has_side_effects=True, vmem_limit_bytes=58 * 1024 * 1024
        ),
    )(
        tokens.reshape(total, part), w_query, keyval, norm_gain.reshape(1, -1), lens, cosine, sine,
        place,
    )


def score_kernel(
    context, pooled, onehot, w_out, members_in, live, returned, members,
    own_rows, own_pooled, all_rows, all_pooled, exact, parts, others, sums, rows_in, joined,
    squares, replies, arrived,
    a_send, a_recv, c_send, c_recv, d_send, d_recv, f_send, f_recv, l_sem,
):
    dp = lax.axis_index("dp")
    mp = lax.axis_index("mp")
    load = pltpu.make_async_copy(members_in, members, l_sem)
    load.start()
    barrier = pltpu.get_barrier_semaphore()
    for i in range(8):
        for j in range(4):
            if i or j:
                pl.semaphore_signal(
                    barrier, inc=1, device_id={"dp": (dp + i) % 8, "mp": (mp + j) % 4},
                    device_id_type=MESH,
                )

    for o in range(8):
        own_pooled[o] = jnp.dot(
            onehot[...], pooled[o], preferred_element_type=jnp.float32
        ).astype(jnp.bfloat16)
    own_rows[...] = jnp.dot(
        onehot[...], context[...].astype(jnp.bfloat16), preferred_element_type=jnp.float32
    ).astype(jnp.bfloat16)
    pl.semaphore_wait(barrier, 31)

    def remote(source, target, send, recv, dp_to, mp_to):
        return pltpu.make_async_remote_copy(
            src_ref=source, dst_ref=target, send_sem=send, recv_sem=recv,
            device_id={"dp": dp_to, "mp": mp_to}, device_id_type=MESH,
        )

    def rows_copy(i, slot):
        return remote(
            own_rows, all_rows.at[slot], a_send.at[0, i], a_recv.at[0, slot], (dp + i) % 8, mp
        )

    def pooled_copy(i, slot):
        to = (dp + i) % 8
        return remote(
            own_pooled.at[to], all_pooled.at[slot], a_send.at[1, i], a_recv.at[1, slot], to, mp
        )

    for i in range(1, 8):
        rows_copy(i, dp).start()
    for i in range(1, 8):
        pooled_copy(i, dp).start()
    all_rows[dp] = own_rows[...]
    all_pooled[dp] = own_pooled[dp]

    load.wait()

    @pl.loop(0, members.shape[0] // 64)
    def _(step):
        rows = pl.ds(pl.multiple_of(step * 64, 64), 64)
        values = members[rows, :].astype(jnp.float32)
        squares[rows, :] = jnp.broadcast_to(
            jnp.sum(values * values, axis=-1, keepdims=True), (64, 128)
        )

    scale = live[...] * lax.rsqrt(squares[...].T[0:1, :] + 1e-06)
    row = lax.broadcasted_iota(jnp.int32, (256, 256), 0)
    column = lax.broadcasted_iota(jnp.int32, (256, 256), 1)
    target = ((row >> 2) & 7) * 32 + (row >> 5) * 4 + (row & 3)
    order = jnp.where(column == target, 1.0, 0.0).astype(jnp.bfloat16)
    for i in range(1, 8):
        rows_copy(i, (dp + i) % 8).wait_recv()
    sorted_rows = jnp.dot(
        order, all_rows[...].reshape(256, -1), preferred_element_type=jnp.float32
    ).astype(jnp.bfloat16)
    product = jnp.dot(sorted_rows, w_out[...], preferred_element_type=jnp.float32)
    parts[...] = product.astype(jnp.bfloat16).reshape(parts.shape)

    def part_copy(i, slot):
        to = (mp + i) % 4
        return remote(parts.at[to], others.at[slot], c_send.at[i], c_recv.at[slot], dp, to)

    for i in range(1, 4):
        part_copy(i, mp).start()
    for i in range(1, 8):
        pooled_copy(i, (dp + i) % 8).wait_recv()
    exact[...] = (
        product
        + jnp.dot(order, all_pooled[...].reshape(256, -1), preferred_element_type=jnp.float32)
    ).reshape(exact.shape)
    total = exact[mp]
    for i in range(1, 4):
        slot = (mp + i) % 4
        part_copy(i, slot).wait_recv()
        total = total + others[slot].astype(jnp.float32)
    sums[...] = total.astype(jnp.bfloat16).reshape(sums.shape)

    def sum_copy(j, i, slot):
        return remote(
            sums.at[j], rows_in.at[slot], d_send.at[j, i], d_recv.at[slot],
            2 * mp + j, (mp + i) % 4,
        )

    for j in range(2):
        mine = 2 * mp + j == dp

        @pl.when(jnp.logical_not(mine))
        def _():
            sum_copy(j, 0, dp).start()

        for i in range(1, 4):
            sum_copy(j, i, dp).start()

        @pl.when(mine)
        def _():
            rows_in[dp] = sums[j]

    for slot in range(8):
        @pl.when(jnp.logical_not((dp // 2 == mp) & (dp == slot)))
        def _():
            sum_copy(0, 0, slot).wait_recv()

    width = rows_in.shape[2]
    for slot in range(8):
        joined[:, slot * width : (slot + 1) * width] = rows_in[slot].astype(jnp.float32)
    embedding = joined[...]
    unit = embedding * lax.rsqrt(jnp.sum(embedding * embedding, axis=-1, keepdims=True) + 1e-06)
    dots = lax.dot_general(
        unit.astype(jnp.bfloat16), members[...], (((1,), (1,)), ((), ())),
        preferred_element_type=jnp.float32,
    )
    found = (dots * scale).astype(jnp.bfloat16)
    row = lax.broadcasted_iota(jnp.int32, (128, 32), 0)
    column = lax.broadcasted_iota(jnp.int32, (128, 32), 1)
    spread = jnp.where(((row & 15) < 4) & (column == (row >> 4) * 4 + (row & 15)), 1.0, 0.0)
    replies[...] = jnp.dot(
        spread.astype(jnp.bfloat16), found, preferred_element_type=jnp.float32
    ).astype(jnp.bfloat16).reshape(replies.shape)

    def reply_copy(i, slot):
        to = (dp + i) % 8
        return remote(replies.at[to], arrived.at[slot], f_send.at[i], f_recv.at[slot], to, mp)

    for i in range(1, 8):
        reply_copy(i, dp).start()
    arrived[dp] = replies[dp]
    for i in range(1, 8):
        reply_copy(i, (dp + i) % 8).wait_recv()
    returned[...] = arrived[...]

    for i in range(1, 8):
        rows_copy(i, dp).wait_send()
        pooled_copy(i, dp).wait_send()
        reply_copy(i, dp).wait_send()
    for i in range(1, 4):
        part_copy(i, mp).wait_send()
    for j in range(2):
        @pl.when(2 * mp + j != dp)
        def _():
            sum_copy(j, 0, dp).wait_send()

        for i in range(1, 4):
            sum_copy(j, i, dp).wait_send()


def score(pooled_context, pooled_input, w_out, members, onehot, live):
    dialogs, head_width = pooled_context.shape
    width = w_out.shape[1]
    member_count = members.shape[0]
    slots = onehot.reshape(-1, dialogs).astype(jnp.bfloat16)
    vmem = pl.BlockSpec(memory_space=pltpu.VMEM)
    half, full = jnp.bfloat16, jnp.float32
    returned = pl.pallas_call(
        score_kernel,
        out_shape=jax.ShapeDtypeStruct((8, 16, member_count), half),
        in_specs=[vmem] * 4 + [pl.BlockSpec(memory_space=pltpu.HBM), vmem],
        out_specs=vmem,
        scratch_shapes=[
            pltpu.VMEM(members.shape, half),
            pltpu.VMEM((32, head_width), half),
            pltpu.VMEM((8, 32, width), half),
            pltpu.VMEM((8, 32, head_width), half),
            pltpu.VMEM((8, 32, width), half),
            pltpu.VMEM((4, 64, width), full),
            pltpu.VMEM((4, 64, width), half),
            pltpu.VMEM((4, 64, width), half),
            pltpu.VMEM((2, 32, width), half),
            pltpu.VMEM((8, 32, width), half),
            pltpu.VMEM((32, 8 * width), full),
            pltpu.VMEM((member_count, 128), full),
            pltpu.VMEM((8, 16, member_count), half),
            pltpu.VMEM((8, 16, member_count), half),
            pltpu.SemaphoreType.DMA((2, 8)),
            pltpu.SemaphoreType.DMA((2, 8)),
            pltpu.SemaphoreType.DMA((4,)),
            pltpu.SemaphoreType.DMA((4,)),
            pltpu.SemaphoreType.DMA((2, 4)),
            pltpu.SemaphoreType.DMA((8,)),
            pltpu.SemaphoreType.DMA((8,)),
            pltpu.SemaphoreType.DMA((8,)),
            pltpu.SemaphoreType.DMA,
        ],
        compiler_params=pltpu.CompilerParams(
            collective_id=1, has_side_effects=True, vmem_limit_bytes=32 * 1024 * 1024
        ),
    )(pooled_context, pooled_input, slots, w_out, members, live)
    return returned[:, : onehot.shape[1]]


def plain_project(tokens, norm_gain, w_query, w_keyval, lengths):
    gathered = lax.all_gather(tokens, "mp", axis=2, tiled=True)
    dialogs, seq_len, width = gathered.shape
    hidden = gathered.astype(jnp.float32)
    normed = (
        hidden * lax.rsqrt(jnp.mean(hidden * hidden, axis=-1, keepdims=True) + 1e-06) * norm_gain
    ).astype(jnp.bfloat16)
    normed_flat = normed.reshape(dialogs * seq_len, width)
    query_cols = w_query.shape[1]
    keyval_cols = w_keyval.shape[2]
    pieces = (
        lax.all_gather(w_query, "dp", axis=0, tiled=True),
        lax.all_gather(w_keyval, "dp", axis=0, tiled=True),
    )
    keyval_piece = pieces[1].reshape(pieces[1].shape[0], 2 * keyval_cols)
    query_sum = jnp.dot(normed_flat, pieces[0], preferred_element_type=jnp.float32)
    keyval_sum = jnp.dot(normed_flat, keyval_piece, preferred_element_type=jnp.float32)
    positions = jnp.arange(seq_len)
    local_heads = query_cols // HEAD_DIM
    local_kv = keyval_cols // HEAD_DIM
    query = jax.vmap(lambda block: rotate(block, positions))(
        query_sum.reshape(dialogs, seq_len, local_heads, HEAD_DIM)
    ).astype(jnp.bfloat16)
    keys = jax.vmap(lambda block: rotate(block, positions))(
        keyval_sum[:, :keyval_cols].reshape(dialogs, seq_len, local_kv, HEAD_DIM)
    ).astype(jnp.bfloat16)
    values = (
        keyval_sum[:, keyval_cols:]
        .reshape(dialogs, seq_len, local_kv, HEAD_DIM)
        .astype(jnp.bfloat16)
    )
    valid = (positions[None, :] < lengths[:, None]).astype(jnp.float32)
    pooled_input = (
        jnp.sum(hidden * valid[:, :, None], axis=1) / lengths.astype(jnp.float32)[:, None]
    )
    pooled_context = jax.vmap(attend)(query, keys, values, lengths).astype(jnp.bfloat16)
    return pooled_context, pooled_input


def plain_score(pooled_context, pooled_input, w_out, members, onehot, live):
    dialogs = pooled_context.shape[0]
    everyone = lax.all_gather(pooled_context, "dp", axis=0, tiled=True)
    slices = jnp.dot(everyone, w_out, preferred_element_type=jnp.float32).astype(jnp.bfloat16)
    slices = slices.reshape(-1, dialogs, w_out.shape[1])
    slices = lax.all_to_all(slices, "dp", split_axis=0, concat_axis=0, tiled=True)
    partial_out = slices.transpose(1, 0, 2).reshape(dialogs, -1)
    projected = lax.psum(partial_out, "mp").astype(jnp.float32)
    embedding = pooled_input + projected
    unit = embedding * lax.rsqrt(jnp.sum(embedding * embedding, axis=-1, keepdims=True) + 1e-06)
    unit = unit.astype(jnp.bfloat16)
    inverse_norm = lax.rsqrt(
        jnp.einsum("md,md->m", members, members, preferred_element_type=jnp.float32) + 1e-06
    )
    outgoing = jnp.einsum(
        "ocn,nd->ocd", onehot.astype(jnp.bfloat16), unit, preferred_element_type=jnp.float32
    ).astype(jnp.bfloat16)
    query_rows = lax.all_to_all(outgoing, "dp", split_axis=0, concat_axis=0, tiled=True)
    dots = lax.dot_general(
        query_rows,
        members,
        (((query_rows.ndim - 1,), (1,)), ((), ())),
        preferred_element_type=jnp.float32,
    )
    return lax.all_to_all(
        jnp.where(live[0] > 0, live[0] * dots * inverse_norm, 0.0).astype(jnp.bfloat16),
        "dp",
        split_axis=0,
        concat_axis=0,
        tiled=True,
    )


def local(
    tokens, norm_gain, w_query, w_keyval, w_out, residents, lengths, cluster, owner, counts, flags
):
    fast = lax.axis_size("dp") == 8 and lax.axis_size("mp") == 4
    if fast:
        project = gather_project
    else:
        project = plain_project
    pooled_context, pooled_input = project(tokens, norm_gain, w_query, w_keyval, lengths)
    dialogs = tokens.shape[0]
    my_index = lax.axis_index("dp")
    owner_count = lax.axis_size("dp")
    my_count = jnp.sum(jnp.where(owner == my_index, counts, 0))
    members = residents[0]
    member_count = members.shape[0]
    member_start = lax.axis_index("mp") * member_count
    live = jnp.where(member_start + jnp.arange(member_count) < my_count, logit_scale, 0.0)[None, :]
    table_size = owner.shape[0]
    cluster_ids = cluster[:, 0]
    destination = jnp.sum(
        jnp.where(jnp.arange(table_size)[None, :] == cluster_ids[:, None], owner[None, :], 0),
        axis=1,
    )
    capacity = max(1, -(-dialogs // owner_count))
    order = jnp.arange(dialogs)
    earlier = (destination[None, :] == destination[:, None]) & (order[None, :] < order[:, None])
    rank = jnp.sum(earlier.astype(jnp.int32), axis=1)
    onehot = (jnp.arange(owner_count)[:, None, None] == destination[None, None, :]) & (
        jnp.arange(capacity)[None, :, None] == rank[None, None, :]
    )
    if fast:
        assign = score
    else:
        assign = plain_score
    returned = assign(pooled_context, pooled_input, w_out, members, onehot, live)
    similarity = jnp.einsum(
        "ocn,ocm->nm", onehot.astype(jnp.bfloat16), returned, preferred_element_type=jnp.float32
    )
    return similarity * flags.astype(jnp.float32)[:, None]


def solution(mesh):
    in_specs = (
        P("dp", None, "mp"),
        P(),
        P("dp", "mp"),
        P("dp", None, "mp"),
        P("mp", "dp"),
        P("dp", "mp"),
        P("dp"),
        P("dp"),
        P(),
        P(),
        P("dp"),
    )
    out_specs = P("dp", "mp")
    return jax.shard_map(local, mesh=mesh, in_specs=in_specs, out_specs=out_specs, check_vma=False)
```
